512 devices in a mesh: seq: 64 (over z, x), batch: 8 (over y, core).
Axes of the slice: x: 4, y: 4, z: 16, core: 2. Of those that a mesh axis runs over, the one named last changes fastest.
Arguments:
- inputs: bfloat16 [8, 8192, 256], P('batch', 'seq'), may hold values from -6 to 6
- cotangent: bfloat16 [8, 8192, 256], P('batch', 'seq'), may hold values from -6 to 6
- decay_rate: float32 [32, 256], replicated, as said below
- rotation: float32 [32, 256], replicated, may hold values from -3.140625 to 3.140625
- readout: float32 [2, 32, 256], replicated, may hold values from -1.5 to 1.5
- skip_gain: float32 [256], replicated, may hold values from -4 to 4
- projection: bfloat16 [256, 256], replicated, may hold values from -0.375 to 0.375
Outputs:
- outputs: bfloat16 [8, 8192, 256], P('batch', 'seq')
- input_grad: bfloat16 [8, 8192, 256], P('batch', 'seq')
- proj_grad: float32 [256, 256], replicated
- readout_grad: float32 [2, 32, 256], replicated
- skip_grad: float32 [256], replicated
The draws below stay inside these ranges and needn't reach their ends.
Inputs may be any that keep to these rules, and one draw needn't show every extreme that they name: `decay_rate`: every decay rate is positive.
All inputs are finite; a program needn't handle non-finite values.
Results may differ from the reference program's by a relative error of at most 0.004.
Values sent between devices are 32-bit elements; how exact they have to be, the bound alone decides.
A program may use at most 128 MiB of HBM per device.

```python
import math
from functools import partial
import jax
import jax.numpy as jnp
from jax import lax

H = 256
N = 32
BLOCK = 16
SEQLEN = 8192
CLIPS = 8


def draw_decay_rate(key, part):
    key_mix, key_slow, key_fast = jax.random.split(key, 3)
    slow_share = 0.5
    slow_mask = jax.random.uniform(key_mix, (N, H)) < slow_share
    slow_rate = jnp.exp(jax.random.uniform(key_slow, (N, H), minval=math.log(0.02 / SEQLEN), maxval=math.log(2.0 / SEQLEN)))
    fast_rate = jnp.exp(jax.random.uniform(key_fast, (N, H), minval=math.log(0.02), maxval=math.log(0.099)))
    return jnp.where(slow_mask, slow_rate, fast_rate).astype(jnp.float32)


def levels(stream_key, extent, cuts, smallest, top_value):
    def one(dim, blocks):
        steps = jax.random.uniform(jax.random.fold_in(jax.random.fold_in(stream_key, 6), dim), (blocks,), jnp.float32, smallest / len(cuts), top_value / len(cuts))
        return jnp.repeat(jnp.exp(steps), extent[dim] // blocks).reshape((-1,) + (1,) * (len(extent) - dim - 1))

    factor_of = one(*cuts[0])
    for cut in cuts[1:]:
        factor_of = factor_of * one(*cut)
    return factor_of


def gaussian(key, extent, deviation, most, shards=(), kind=jnp.bfloat16):
    entries = deviation * jax.random.normal(key, extent, jnp.float32)
    if shards:
        entries = entries * levels(key, extent, shards, -0.22, 0.18)
    return jnp.clip(entries, -most, most).astype(kind)


def setup_inputs(seed: int = 0) -> dict:
    key_list = jax.random.split(jax.random.key(seed), 8)
    return {
        "inputs": gaussian(key_list[0], (CLIPS, SEQLEN, H), 1.0, 6.0, ((0, 8), (1, 64))),
        "cotangent": gaussian(key_list[1], (CLIPS, SEQLEN, H), 1.0, 6.0, ((0, 8), (1, 64))),
        "decay_rate": draw_decay_rate(jax.random.fold_in(key_list[7], 71), 0),
        "rotation": jnp.clip(jax.random.uniform(key_list[3], (N, H), jnp.float32, -3.140625, 3.140625), -3.140625, 3.140625),
        "readout": gaussian(key_list[4], (2, N, H), 0.25, 1.5, (), jnp.float32),
        "skip_gain": gaussian(key_list[5], (H,), 1.0, 4.0, (), jnp.float32),
        "projection": gaussian(key_list[6], (H, H), H ** -0.5, 0.375),
    }


PRECISE = lax.Precision.HIGHEST

def contract(form, table, data):
    return jnp.einsum(form, table, data, precision=PRECISE)

def complex_mul(left_re, left_im, right_re, right_im):
    return (left_re * right_re - left_im * right_im, left_re * right_im + left_im * right_re)

def powers(decay_rate, rotation, block_len):
    exponents = jnp.arange(block_len + 1).astype(jnp.float32)[:, None, None]
    magnitude = jnp.exp(-decay_rate[None] * exponents)
    return (magnitude * jnp.cos(rotation[None] * exponents), magnitude * jnp.sin(rotation[None] * exponents))

def kernels(pow_re, pow_im, readout, in_gain, block_len):
    kernel = lax.optimization_barrier(jnp.sum(in_gain * (readout[0] * pow_re[:block_len] - readout[1] * pow_im[:block_len]), axis=1))
    positions = jnp.arange(block_len)
    lag_index = positions[:, None] - positions[None, :]
    toeplitz = jnp.where((lag_index >= 0)[:, :, None], kernel[jnp.clip(lag_index, 0, block_len - 1)], 0.0)
    diag_table = (lag_index[:, :, None] == positions[None, None, :]).astype(jnp.float32)
    return (toeplitz, diag_table)

def reference(inputs, cotangent, decay_rate, rotation, readout, skip_gain, projection):
    clip_count, length, channels = inputs.shape
    block_len = BLOCK
    blocks = length // block_len
    pow_re, pow_im = powers(decay_rate, rotation, block_len)
    in_gain = jnp.sqrt(-jnp.expm1(-2.0 * decay_rate))
    toeplitz, diag_table = kernels(pow_re, pow_im, readout, in_gain, block_len)
    step_re, step_im = (pow_re[block_len], pow_im[block_len])
    segments = inputs.astype(jnp.float32).reshape(clip_count, blocks, block_len, channels).transpose(1, 0, 2, 3)

    def forward(carried, segment):
        state_re, state_im = carried
        mixed_re, mixed_im = complex_mul(readout[0], readout[1], state_re, state_im)
        within = contract('jnh,cnh->cjh', pow_re[1:], mixed_re) - contract('jnh,cnh->cjh', pow_im[1:], mixed_im)
        within = within + contract('jsh,csh->cjh', toeplitz, segment) + skip_gain * segment
        fill_re = in_gain * contract('snh,csh->cnh', pow_re[block_len - 1::-1], segment)
        fill_im = in_gain * contract('snh,csh->cnh', pow_im[block_len - 1::-1], segment)
        new_re, new_im = complex_mul(step_re, step_im, state_re, state_im)
        return ((new_re + fill_re, new_im + fill_im), within)
    zeros_state = jnp.zeros((clip_count,) + decay_rate.shape, jnp.float32)
    _, mixed_out = lax.scan(forward, (zeros_state, zeros_state), segments)
    mixed_out = mixed_out.transpose(1, 0, 2, 3).reshape(clip_count * length, channels)
    hidden = jax.nn.gelu(mixed_out, approximate=True).astype(jnp.bfloat16)
    flat_in = inputs.reshape(clip_count * length, channels)
    outputs = (flat_in.astype(jnp.float32) + jnp.dot(hidden, projection, preferred_element_type=jnp.float32)).astype(jnp.bfloat16)
    flat_tan = cotangent.reshape(clip_count * length, channels)
    proj_part = jnp.dot(hidden.T, flat_tan, preferred_element_type=jnp.float32)
    hidden_back = jnp.dot(flat_tan, projection.T, preferred_element_type=jnp.float32)
    _, gelu_back = jax.vjp(partial(jax.nn.gelu, approximate=True), mixed_out)
    mixed_grad = gelu_back(hidden_back)[0]
    grad_segments = mixed_grad.reshape(clip_count, blocks, block_len, channels).transpose(1, 0, 2, 3)

    def backward(carried, paired):
        next_re, next_im, acc_re, acc_im, correlation = carried
        grad_segment, segment = paired
        weighted_re, weighted_im = complex_mul(readout[0], readout[1], in_gain * next_re, in_gain * next_im)
        within = contract('snh,cnh->csh', pow_re[block_len:0:-1], weighted_re) - contract('snh,cnh->csh', pow_im[block_len:0:-1], weighted_im)
        within = within + contract('jsh,cjh->csh', toeplitz, grad_segment) + skip_gain * grad_segment
        lead_re = contract('snh,csh->cnh', pow_re[block_len:0:-1], segment)
        lead_im = contract('snh,csh->cnh', pow_im[block_len:0:-1], segment)
        prod_re, prod_im = complex_mul(lead_re, lead_im, next_re, next_im)
        acc_re = acc_re + in_gain * lax.optimization_barrier(jnp.sum(prod_re, axis=0))
        acc_im = acc_im + in_gain * lax.optimization_barrier(jnp.sum(prod_im, axis=0))
        correlation = correlation + contract('cjh,csh->jsh', grad_segment, segment)
        fresh_re = contract('jnh,cjh->cnh', pow_re[:block_len], grad_segment)
        fresh_im = contract('jnh,cjh->cnh', pow_im[:block_len], grad_segment)
        new_re, new_im = complex_mul(step_re, step_im, next_re, next_im)
        return ((new_re + fresh_re, new_im + fresh_im, acc_re, acc_im, correlation), within)
    zeros_acc = jnp.zeros(decay_rate.shape, jnp.float32)
    zeros_corr = jnp.zeros((block_len, block_len, channels), jnp.float32)
    carried, back_within = lax.scan(backward, (zeros_state, zeros_state, zeros_acc, zeros_acc, zeros_corr), (grad_segments, segments), reverse=True)
    acc_re, acc_im, correlation = (carried[2], carried[3], carried[4])
    back_within = back_within.transpose(1, 0, 2, 3).reshape(clip_count * length, channels)
    input_grad = (back_within + flat_tan.astype(jnp.float32)).reshape(clip_count, length, channels).astype(jnp.bfloat16)
    lag_sum = jnp.einsum('jsh,jsd->dh', correlation, diag_table, precision=PRECISE)
    acc_re = acc_re + in_gain * jnp.einsum('dnh,dh->nh', pow_re[:block_len], lag_sum, precision=PRECISE)
    acc_im = acc_im + in_gain * jnp.einsum('dnh,dh->nh', pow_im[:block_len], lag_sum, precision=PRECISE)
    readout_part = jnp.stack([acc_re, -acc_im])
    skip_part = lax.optimization_barrier(jnp.sum(mixed_grad * flat_in.astype(jnp.float32), axis=0))
    squares = jnp.sum(proj_part * proj_part) + jnp.sum(readout_part * readout_part) + jnp.sum(skip_part * skip_part)
    params = channels * channels + 2 * decay_rate.shape[0] * channels + channels
    ceiling = math.sqrt(params)
    factor = jnp.minimum(1.0, ceiling / (jnp.sqrt(squares) + 1e-06))
    return (outputs.reshape(clip_count, length, channels), input_grad, factor * proj_part, factor * readout_part, factor * skip_part)
```

```python
import math

import jax
import jax.numpy as jnp
import numpy as np
from jax import lax
from jax.experimental import pallas as pl
from jax.experimental.pallas import tpu as pltpu
from jax.sharding import PartitionSpec as P

MESH = pl.DeviceIdType.MESH
F32 = jnp.float32
STATES, CHANNELS, RUN = 32, 256, 128
GROUP = 8
BLOCKS = 8
OWNERS = 32

TURN_HI = 6.28125
TURN_MID = round((2 * math.pi - TURN_HI) * 2**20) / 2**20
TURN_LO = 2 * math.pi - TURN_HI - TURN_MID
GELU_SCALE = math.sqrt(2 / math.pi)
GELU_CUBE = 0.044715
CEILING = math.sqrt(CHANNELS * CHANNELS + 2 * STATES * CHANNELS + CHANNELS)


def cmul(a, b):
    return a[0] * b[0] - a[1] * b[1], a[0] * b[1] + a[1] * b[0]


def decay_power(decay, rotation, times):
    angle = rotation * float(times)
    if times > 1:
        turns = jnp.floor(angle * (0.5 / math.pi) + 0.5)
        angle = ((angle - turns * TURN_HI) - turns * TURN_MID) - turns * TURN_LO
    size = jnp.exp(decay * -float(times))
    return size * jnp.cos(angle), size * jnp.sin(angle)


def entry_gain(decay):
    y = 2.0 * decay
    series = 1.0 - y * (1.0 / 8)
    for k in (7, 6, 5, 4, 3, 2):
        series = 1.0 - y * (1.0 / k) * series
    return jnp.sqrt(jnp.where(y < 0.25, y * series, 1.0 - jnp.exp(-y)))


def put_pieces(ref, value):
    re, im = value
    for p in range(GROUP):
        rows, cols = slice(8 * (p // 2), 8 * (p // 2) + 8), slice(128 * (p % 2), 128 * (p % 2) + 128)
        ref[p, 0:8, :] = re[rows, cols]
        ref[p, 8:16, :] = im[rows, cols]


def get_pieces(ref):
    def part(lo):
        return jnp.concatenate(
            [
                jnp.concatenate([ref[2 * n, lo : lo + 8, :], ref[2 * n + 1, lo : lo + 8, :]], axis=1)
                for n in range(4)
            ],
            axis=0,
        )

    return part(0), part(8)


def load(ref, i):
    return ref[i, 0:8, :], ref[i, 8:16, :]


def store(ref, i, value):
    ref[i, 0:8, :] = value[0]
    ref[i, 8:16, :] = value[1]


def kernel(
    x_ref, cot_ref, decay_ref, rot_ref, read_ref, skip_ref, proj_ref,
    out_ref, ig_ref, pg_ref, rg_ref, sg_ref,
    xf, gf, mix, hb, il,
    lam_s, cof_s, l128, l1024,
    e_buf, o_buf, t_buf, r1f, r2f, hin, r1b, r2b, lin,
    pb, gb, ra1p, ra1g, a2s, ra2, pc, ra3, full,
    ssem, rsem,
):
    s, b = lax.axis_index("seq"), lax.axis_index("batch")
    g, blk = lax.rem(s, GROUP), lax.div(s, GROUP)
    y, c = lax.div(b, 2), lax.rem(b, 2)
    me = lax.div(g, 4) * 16 + lax.rem(g, 4) * 4 + y

    def in_block(k):
        return {"seq": blk * GROUP + lax.rem(g + k, GROUP), "batch": b}

    def across(k):
        return {"seq": lax.rem(blk + k, BLOCKS) * GROUP + g, "batch": b}

    def owner(k):
        o = lax.rem(me + k, OWNERS)
        seq = blk * GROUP + lax.div(o, 16) * 4 + lax.div(lax.rem(o, 16), 4)
        return o, {"seq": seq, "batch": lax.rem(o, 4) * 2 + c}

    other = {"seq": s, "batch": y * 2 + (1 - c)}

    barrier = pltpu.get_barrier_semaphore()
    partners = [across(k) for k in range(1, BLOCKS)]
    partners += [owner(k)[1] for k in range(1, OWNERS)] + [other]
    partners_n = len(partners)
    for device in partners:
        pl.semaphore_signal(barrier, inc=1, device_id=device, device_id_type=MESH)

    def copy(src, dst, n, device):
        return pltpu.make_async_remote_copy(
            src_ref=src, dst_ref=dst, send_sem=ssem.at[n], recv_sem=rsem.at[n],
            device_id=device, device_id_type=MESH,
        )

    decay, rot = decay_ref[...], rot_ref[...]
    gain = entry_gain(decay)
    lam = decay_power(decay, rot, 1)
    put_pieces(l128, decay_power(decay, rot, RUN))
    put_pieces(l1024, decay_power(decay, rot, RUN * GROUP))
    lam_s[0], lam_s[1] = lam
    cof_s[0] = gain * read_ref[0]
    cof_s[1] = gain * read_ref[1]
    xf[...] = x_ref[...].astype(F32)
    row_id = lax.broadcasted_iota(jnp.int32, (8, CHANNELS), 0)
    zero = jnp.zeros((STATES, CHANNELS), F32)

    def sweep(carry, body, backward=False):
        def step(i, carry):
            first = RUN - 8 - 8 * i if backward else 8 * i
            first = pl.multiple_of(first, 8)
            return body(first, carry)

        return lax.fori_loop(0, RUN // 8, step, carry)

    order = tuple(range(8))

    def fwd_local(first, carry):
        lam_re, lam_im = lam_s[0], lam_s[1]
        cof_re, cof_im = cof_s[0], cof_s[1]
        rows = xf[pl.ds(first, 8), :]
        re, im = carry
        acc = jnp.zeros((8, CHANNELS), F32)
        for j in order:
            re, im = lam_re * re - lam_im * im + rows[j : j + 1, :], lam_re * im + lam_im * re
            total = jnp.sum(cof_re * re - cof_im * im, axis=0, keepdims=True)
            acc = jnp.where(row_id == j, total, acc)
        mix[pl.ds(first, 8), :] = acc + rows * skip_ref[...]
        return re, im

    re, im = sweep((zero, zero), fwd_local)
    put_pieces(e_buf, (gain * re, gain * im))
    hb[...] = lax.dot_general(
        cot_ref[...], proj_ref[...], (((1,), (1,)), ((), ())), preferred_element_type=F32
    )
    pl.semaphore_wait(barrier, partners_n)

    sends = []

    def scatter(buf, dst, n):
        dst[g] = buf[g]
        for k in range(1, GROUP):
            p = lax.rem(g + k, GROUP)
            copy(buf.at[p], dst.at[g], n, in_block(k)).start()
        sends.append((buf.at[pl.ds(0, GROUP - 1)], n))

    def spread(src, dst, n):
        dst[blk] = src[...]
        for k in range(1, BLOCKS):
            copy(src, dst.at[blk], n, across(k)).start()
        sends.append((dst.at[pl.ds(0, BLOCKS - 1)], n))

    def arrive(ref, n):
        copy(ref, ref, n, other).wait_recv()

    def block_total(r1, turn):
        step = load(l128, g)
        total = load(r1, turn[0])
        for i in turn[1:]:
            moved = cmul(step, total)
            nxt = load(r1, i)
            total = moved[0] + nxt[0], moved[1] + nxt[1]
        return total

    def entering(r1, r2, buf, turn, backward):
        step, leap = load(l128, g), load(l1024, g)
        state = (jnp.zeros((8, 128), F32), jnp.zeros((8, 128), F32))
        for i in turn:
            moved, nxt = cmul(leap, state), load(r2, i)
            use = (i > blk) if backward else (i < blk)
            state = tuple(jnp.where(use, m + v, old) for m, v, old in zip(moved, nxt, state))
        for i in turn:
            store(buf, i, state)
            moved, nxt = cmul(step, state), load(r1, i)
            state = moved[0] + nxt[0], moved[1] + nxt[1]

    up, down = tuple(range(8)), tuple(range(7, -1, -1))
    seven = pl.ds(0, 7)

    scatter(e_buf, r1f, 0)
    arrive(r1f.at[seven], 0)
    t = block_total(r1f, up)
    t_buf[0, 0:8, :], t_buf[0, 8:16, :] = t
    spread(t_buf.at[0], r2f, 1)
    arrive(r2f.at[seven], 1)
    entering(r1f, r2f, o_buf.at[0], up, False)
    scatter(o_buf.at[0], hin, 2)
    arrive(hin.at[seven], 2)

    enter = get_pieces(hin)
    carried = cmul((read_ref[0], read_ref[1]), enter)

    def fwd_inject(first, carry):
        lam_re, lam_im = lam_s[0], lam_s[1]
        re, im = carry
        acc = jnp.zeros((8, CHANNELS), F32)
        for j in order:
            re, im = lam_re * re - lam_im * im, lam_re * im + lam_im * re
            acc = jnp.where(row_id == j, jnp.sum(re, axis=0, keepdims=True), acc)
        mix[pl.ds(first, 8), :] = mix[pl.ds(first, 8), :] + acc
        return re, im

    sweep(carried, fwd_inject)

    mixed = mix[...]
    square = mixed * mixed
    tanh = jnp.tanh(GELU_SCALE * (mixed + GELU_CUBE * (mixed * square)))
    half = 0.5 * (1.0 + tanh)
    hidden = (mixed * half).astype(jnp.bfloat16)
    slope = half + (0.5 * mixed) * (1.0 - tanh * tanh) * (
        GELU_SCALE * (1.0 + (3.0 * GELU_CUBE) * square)
    )
    grad = hb[...] * slope
    gf[...] = grad
    part = lax.dot_general(
        hidden, cot_ref[...], (((0,), (0,)), ((), ())), preferred_element_type=F32
    )
    for half_id in range(2):
        for o in range(OWNERS):
            pb[half_id, o] = part[8 * o : 8 * o + 8, 128 * half_id : 128 * half_id + 128]
    copy(pb.at[1 - c], ra1p, 3, other).start()
    sends.append((pb.at[0], 3))

    def bwd_local(first, carry):
        lam_re, lam_im = lam_s[0], lam_s[1]
        rows, xs = gf[pl.ds(first, 8), :], xf[pl.ds(first, 8), :]
        re, im, sum_re, sum_im = carry
        for j in reversed(order):
            re, im = lam_re * re - lam_im * im + rows[j : j + 1, :], lam_re * im + lam_im * re
            sum_re = sum_re + xs[j : j + 1, :] * re
            sum_im = sum_im + xs[j : j + 1, :] * im
        return re, im, sum_re, sum_im

    re, im, sum_re, sum_im = sweep((zero, zero, zero, zero), bwd_local, True)
    put_pieces(e_buf.at[pl.ds(GROUP, GROUP)], (re, im))
    scatter(e_buf.at[pl.ds(GROUP, GROUP)], r1b, 4)
    lam = lam_s[0], lam_s[1]
    extra = cmul(cmul(lam, (re, im)), get_pieces(hin))
    read_re = gain * sum_re + extra[0]
    read_im = -(gain * sum_im + extra[1])
    skip_part = jnp.sum(gf[...] * xf[...], axis=0, keepdims=True)
    for half_id in range(2):
        cols = slice(128 * half_id, 128 * half_id + 128)
        for n in range(4):
            gb[half_id, n] = read_re[8 * n : 8 * n + 8, cols]
            gb[half_id, 4 + n] = read_im[8 * n : 8 * n + 8, cols]
        gb[half_id, 8] = jnp.where(row_id[:, :128] == 0, skip_part[:, cols], 0.0)
    copy(gb.at[1 - c], ra1g, 5, other).start()
    sends.append((gb.at[0], 5))
    a2s[...] = jnp.zeros_like(a2s)
    arrive(ra1p, 3)
    for o in range(OWNERS):
        a2s[o, 0:8, :] = pb[c, o] + ra1p[o]
    arrive(ra1g, 5)
    for o in range(9):
        a2s[o, 8:16, :] = gb[c, o] + ra1g[o]
    ra2[me] = a2s[me]
    for k in range(1, OWNERS):
        o, device = owner(k)
        copy(a2s.at[o], ra2.at[me], 6, device).start()
    sends.append((ra2.at[pl.ds(0, OWNERS - 1)], 6))

    out_ref[...] = (
        xf[...] + jnp.dot(hidden, proj_ref[...], preferred_element_type=F32)
    ).astype(jnp.bfloat16)

    arrive(r1b.at[seven], 4)
    t = block_total(r1b, down)
    t_buf[1, 0:8, :], t_buf[1, 8:16, :] = t
    spread(t_buf.at[1], r2b, 7)

    def bwd_read(first, carry):
        lam_re, lam_im = lam_s[0], lam_s[1]
        cof_re, cof_im = cof_s[0], cof_s[1]
        rows = gf[pl.ds(first, 8), :]
        re, im = carry
        acc = jnp.zeros((8, CHANNELS), F32)
        for j in reversed(order):
            re, im = lam_re * re - lam_im * im + rows[j : j + 1, :], lam_re * im + lam_im * re
            total = jnp.sum(cof_re * re - cof_im * im, axis=0, keepdims=True)
            acc = jnp.where(row_id == j, total, acc)
        il[pl.ds(first, 8), :] = acc + rows * skip_ref[...]
        return re, im

    sweep((zero, zero), bwd_read, True)
    il[...] = il[...] + cot_ref[...].astype(F32)

    arrive(ra2.at[pl.ds(0, OWNERS - 1)], 6)
    total = ra2[0]
    for o in range(1, OWNERS):
        total = total + ra2[o]
    pc[0] = total
    spread(pc.at[0], ra3, 8)

    arrive(r2b.at[seven], 7)
    entering(r1b, r2b, o_buf.at[1], down, True)
    scatter(o_buf.at[1], lin, 9)

    arrive(ra3.at[seven], 8)
    total = ra3[0]
    for o in range(1, BLOCKS):
        total = total + ra3[o]
    full[c, me] = total
    for k in range(1, OWNERS):
        copy(full.at[c, me], full.at[c, me], 10, owner(k)[1]).start()
    sends.append((ra2.at[pl.ds(0, OWNERS - 1)], 10))

    arrive(lin.at[seven], 9)
    carried = cmul((cof_s[0], cof_s[1]), get_pieces(lin))

    def bwd_inject(first, carry):
        lam_re, lam_im = lam_s[0], lam_s[1]
        re, im = carry
        acc = jnp.zeros((8, CHANNELS), F32)
        for j in reversed(order):
            re, im = lam_re * re - lam_im * im, lam_re * im + lam_im * re
            acc = jnp.where(row_id == j, jnp.sum(re, axis=0, keepdims=True), acc)
        il[pl.ds(first, 8), :] = il[pl.ds(first, 8), :] + acc
        return re, im

    sweep(carried, bwd_inject, True)
    ig_ref[...] = il[...].astype(jnp.bfloat16)

    arrive(full.at[0, pl.ds(0, OWNERS - 1)], 10)
    copy(full.at[c], full.at[c], 11, other).start()
    sends.append((full.at[0], 11))
    arrive(full.at[0], 11)

    squares = jnp.zeros((16, 128), F32)
    for half_id in range(2):
        for o in range(OWNERS):
            v = full[half_id, o]
            squares = squares + v * v
    norm = jnp.sqrt(jnp.sum(jnp.sum(squares, axis=0, keepdims=True), axis=1, keepdims=True))
    factor = jnp.minimum(1.0, CEILING / (norm + 1e-06))
    for half_id in range(2):
        cols = slice(128 * half_id, 128 * half_id + 128)
        for o in range(OWNERS):
            pg_ref[8 * o : 8 * o + 8, cols] = full[half_id, o, 0:8, :] * factor
        for n in range(4):
            rg_ref[0, 8 * n : 8 * n + 8, cols] = full[half_id, n, 8:16, :] * factor
            rg_ref[1, 8 * n : 8 * n + 8, cols] = full[half_id, 4 + n, 8:16, :] * factor
        sg_ref[:, cols] = full[half_id, 8, 8:9, :] * factor
    for ref, n in sends:
        copy(ref, ref, n, other).wait_send()


def shards(inputs, cotangent, decay_rate, rotation, readout, skip_gain, projection):
    bf16 = jnp.bfloat16
    row, state = (RUN, CHANNELS), (2, STATES, CHANNELS)
    pieces = (GROUP, 16, 128)
    vmem = pl.BlockSpec(memory_space=pltpu.VMEM)
    shapes = [row] * 5 + [state, state, pieces, pieces]
    shapes += [(2 * GROUP, 16, 128), (2,) + pieces, (2, 16, 128)] + [pieces] * 6
    shapes += [(2, OWNERS, 8, 128), (2, 9, 8, 128), (OWNERS, 8, 128), (9, 8, 128)]
    shapes += [(OWNERS, 16, 128), (OWNERS, 16, 128), (1, 16, 128), pieces, (2, OWNERS, 16, 128)]
    outs = pl.pallas_call(
        kernel,
        out_shape=(
            jax.ShapeDtypeStruct(row, bf16),
            jax.ShapeDtypeStruct(row, bf16),
            jax.ShapeDtypeStruct((CHANNELS, CHANNELS), F32),
            jax.ShapeDtypeStruct(state, F32),
            jax.ShapeDtypeStruct((1, CHANNELS), F32),
        ),
        in_specs=[vmem] * 7,
        out_specs=[vmem] * 5,
        scratch_shapes=[pltpu.VMEM(shape, F32) for shape in shapes]
        + [pltpu.SemaphoreType.DMA((12,)), pltpu.SemaphoreType.DMA((12,))],
        compiler_params=pltpu.CompilerParams(
            collective_id=0, has_side_effects=True, vmem_limit_bytes=32 << 20
        ),
        name="layer",
    )(
        inputs[0], cotangent[0], decay_rate, rotation, readout,
        skip_gain.reshape(1, CHANNELS), projection,
    )
    return outs[0][None], outs[1][None], outs[2], outs[3], outs[4].reshape(CHANNELS)


def solution(mesh):
    split = P("batch", "seq", None)
    return jax.shard_map(
        shards,
        mesh=mesh,
        in_specs=(split, split, P(), P(), P(), P(), P()),
        out_specs=(split, split, P(), P(), P()),
        check_vma=False,
    )
```

```python
import math

import jax
import jax.numpy as jnp
import numpy as np
from jax import lax
from jax.experimental import pallas as pl
from jax.experimental.pallas import tpu as pltpu
from jax.sharding import PartitionSpec as P

MESH = pl.DeviceIdType.MESH
F32 = jnp.float32
STATES, CHANNELS, RUN = 32, 256, 128
GROUP = 8
BLOCKS = 8
OWNERS = 32

TURN_HI = 6.28125
TURN_MID = round((2 * math.pi - TURN_HI) * 2**20) / 2**20
TURN_LO = 2 * math.pi - TURN_HI - TURN_MID
GELU_SCALE = math.sqrt(2 / math.pi)
GELU_CUBE = 0.044715
CEILING = math.sqrt(CHANNELS * CHANNELS + 2 * STATES * CHANNELS + CHANNELS)


def cmul(a, b):
    return a[0] * b[0] - a[1] * b[1], a[0] * b[1] + a[1] * b[0]


def decay_power(decay, rotation, times):
    angle = rotation * float(times)
    if times > 1:
        turns = jnp.floor(angle * (0.5 / math.pi) + 0.5)
        angle = ((angle - turns * TURN_HI) - turns * TURN_MID) - turns * TURN_LO
    size = jnp.exp(decay * -float(times))
    return size * jnp.cos(angle), size * jnp.sin(angle)


def entry_gain(decay):
    y = 2.0 * decay
    series = 1.0 - y * (1.0 / 8)
    for k in (7, 6, 5, 4, 3, 2):
        series = 1.0 - y * (1.0 / k) * series
    return jnp.sqrt(jnp.where(y < 0.25, y * series, 1.0 - jnp.exp(-y)))


def put_pieces(ref, value):
    re, im = value
    for p in range(GROUP):
        rows, cols = slice(8 * (p // 2), 8 * (p // 2) + 8), slice(128 * (p % 2), 128 * (p % 2) + 128)
        ref[p, 0:8, :] = re[rows, cols]
        ref[p, 8:16, :] = im[rows, cols]


def get_pieces(ref):
    def part(lo):
        return jnp.concatenate(
            [
                jnp.concatenate([ref[2 * n, lo : lo + 8, :], ref[2 * n + 1, lo : lo + 8, :]], axis=1)
                for n in range(4)
            ],
            axis=0,
        )

    return part(0), part(8)


def load(ref, i):
    return ref[i, 0:8, :], ref[i, 8:16, :]


def store(ref, i, value):
    ref[i, 0:8, :] = value[0]
    ref[i, 8:16, :] = value[1]


def kernel(
    x_hbm, cot_hbm, decay_hbm, rot_hbm, read_hbm, skip_hbm, proj_hbm,
    out_ref, ig_ref, full,
    x_ref, cot_ref, decay_ref, rot_ref, read_ref, skip_ref, proj_ref,
    xf, gf, mix, hb, il,
    lam_s, cof_s, l128, l1024,
    e_buf, o_buf, t_buf, r1f, r2f, hin, r1b, r2b, lin,
    pb, gb, ra1p, ra1g, a2s, ra2, pc, ra3,
    isem, ssem, rsem,
):
    s, b = lax.axis_index("seq"), lax.axis_index("batch")
    g, blk = lax.rem(s, GROUP), lax.div(s, GROUP)
    y, c = lax.div(b, 2), lax.rem(b, 2)
    me = lax.div(g, 4) * 16 + lax.rem(g, 4) * 4 + y

    def in_block(k):
        return {"seq": blk * GROUP + lax.rem(g + k, GROUP), "batch": b}

    def across(k):
        return {"seq": lax.rem(blk + k, BLOCKS) * GROUP + g, "batch": b}

    def owner(k):
        o = lax.rem(me + k, OWNERS)
        seq = blk * GROUP + lax.div(o, 16) * 4 + lax.div(lax.rem(o, 16), 4)
        return o, {"seq": seq, "batch": lax.rem(o, 4) * 2 + c}

    other = {"seq": s, "batch": y * 2 + (1 - c)}

    fetches = [
        pltpu.make_async_copy(src, dst, isem.at[i])
        for i, (src, dst) in enumerate(
            [(decay_hbm, decay_ref), (rot_hbm, rot_ref), (read_hbm, read_ref), (x_hbm, x_ref),
             (skip_hbm, skip_ref), (cot_hbm, cot_ref), (proj_hbm, proj_ref)]
        )
    ]
    for fetch in fetches:
        fetch.start()

    barrier = pltpu.get_barrier_semaphore()
    partners = [across(k) for k in range(1, BLOCKS)]
    partners += [owner(k)[1] for k in range(1, OWNERS)] + [other]
    partners_n = len(partners)
    for device in partners:
        pl.semaphore_signal(barrier, inc=1, device_id=device, device_id_type=MESH)

    def copy(src, dst, n, device):
        return pltpu.make_async_remote_copy(
            src_ref=src, dst_ref=dst, send_sem=ssem.at[n], recv_sem=rsem.at[n],
            device_id=device, device_id_type=MESH,
        )

    for fetch in fetches:
        fetch.wait()

    decay, rot = decay_ref[...], rot_ref[...]
    gain = entry_gain(decay)
    lam = decay_power(decay, rot, 1)
    put_pieces(l128, decay_power(decay, rot, RUN))
    put_pieces(l1024, decay_power(decay, rot, RUN * GROUP))
    lam_s[0], lam_s[1] = lam
    cof_s[0] = gain * read_ref[0]
    cof_s[1] = gain * read_ref[1]
    xf[...] = x_ref[...].astype(F32)
    row_id = lax.broadcasted_iota(jnp.int32, (8, CHANNELS), 0)
    zero = jnp.zeros((STATES, CHANNELS), F32)

    def sweep(carry, body, backward=False):
        def step(i, carry):
            first = RUN - 8 - 8 * i if backward else 8 * i
            first = pl.multiple_of(first, 8)
            return body(first, carry)

        return lax.fori_loop(0, RUN // 8, step, carry)

    order = tuple(range(8))

    def fwd_local(first, carry):
        lam_re, lam_im = lam_s[0], lam_s[1]
        cof_re, cof_im = cof_s[0], cof_s[1]
        rows = xf[pl.ds(first, 8), :]
        re, im = carry
        acc = jnp.zeros((8, CHANNELS), F32)
        for j in order:
            re, im = lam_re * re - lam_im * im + rows[j : j + 1, :], lam_re * im + lam_im * re
            total = jnp.sum(cof_re * re - cof_im * im, axis=0, keepdims=True)
            acc = jnp.where(row_id == j, total, acc)
        mix[pl.ds(first, 8), :] = acc + rows * skip_ref[...]
        return re, im

    re, im = sweep((zero, zero), fwd_local)
    put_pieces(e_buf, (gain * re, gain * im))
    hb[...] = lax.dot_general(
        cot_ref[...], proj_ref[...], (((1,), (1,)), ((), ())), preferred_element_type=F32
    )
    pl.semaphore_wait(barrier, partners_n)

    sends = []

    def scatter(buf, dst, n):
        dst[g] = buf[g]
        for k in range(1, GROUP):
            p = lax.rem(g + k, GROUP)
            copy(buf.at[p], dst.at[g], n, in_block(k)).start()
        sends.append((buf.at[pl.ds(0, GROUP - 1)], n))

    def spread(src, dst, n):
        dst[blk] = src[...]
        for k in range(1, BLOCKS):
            copy(src, dst.at[blk], n, across(k)).start()
        sends.append((dst.at[pl.ds(0, BLOCKS - 1)], n))

    def arrive(ref, n):
        copy(ref, ref, n, other).wait_recv()

    def block_total(r1, turn):
        step = load(l128, g)
        total = load(r1, turn[0])
        for i in turn[1:]:
            moved = cmul(step, total)
            nxt = load(r1, i)
            total = moved[0] + nxt[0], moved[1] + nxt[1]
        return total

    def entering(r1, r2, buf, turn, backward):
        step, leap = load(l128, g), load(l1024, g)
        state = (jnp.zeros((8, 128), F32), jnp.zeros((8, 128), F32))
        for i in turn:
            moved, nxt = cmul(leap, state), load(r2, i)
            use = (i > blk) if backward else (i < blk)
            state = tuple(jnp.where(use, m + v, old) for m, v, old in zip(moved, nxt, state))
        for i in turn:
            store(buf, i, state)
            moved, nxt = cmul(step, state), load(r1, i)
            state = moved[0] + nxt[0], moved[1] + nxt[1]

    up, down = tuple(range(8)), tuple(range(7, -1, -1))
    seven = pl.ds(0, 7)

    scatter(e_buf, r1f, 0)
    arrive(r1f.at[seven], 0)
    t = block_total(r1f, up)
    t_buf[0, 0:8, :], t_buf[0, 8:16, :] = t
    spread(t_buf.at[0], r2f, 1)
    arrive(r2f.at[seven], 1)
    entering(r1f, r2f, o_buf.at[0], up, False)
    scatter(o_buf.at[0], hin, 2)
    arrive(hin.at[seven], 2)

    enter = get_pieces(hin)
    carried = cmul((read_ref[0], read_ref[1]), enter)

    def fwd_inject(first, carry):
        lam_re, lam_im = lam_s[0], lam_s[1]
        re, im = carry
        acc = jnp.zeros((8, CHANNELS), F32)
        for j in order:
            re, im = lam_re * re - lam_im * im, lam_re * im + lam_im * re
            acc = jnp.where(row_id == j, jnp.sum(re, axis=0, keepdims=True), acc)
        mix[pl.ds(first, 8), :] = mix[pl.ds(first, 8), :] + acc
        return re, im

    sweep(carried, fwd_inject)

    mixed = mix[...]
    square = mixed * mixed
    tanh = jnp.tanh(GELU_SCALE * (mixed + GELU_CUBE * (mixed * square)))
    half = 0.5 * (1.0 + tanh)
    hidden = (mixed * half).astype(jnp.bfloat16)
    slope = half + (0.5 * mixed) * (1.0 - tanh * tanh) * (
        GELU_SCALE * (1.0 + (3.0 * GELU_CUBE) * square)
    )
    grad = hb[...] * slope
    gf[...] = grad
    part = lax.dot_general(
        hidden, cot_ref[...], (((0,), (0,)), ((), ())), preferred_element_type=F32
    )
    for half_id in range(2):
        for o in range(OWNERS):
            for q in range(2):
                row = 8 * o + 4 * q
                pb[half_id, o, q] = part[row : row + 4, 128 * half_id : 128 * half_id + 128]
    copy(pb.at[1 - c], ra1p, 3, other).start()
    sends.append((pb.at[0], 3))

    def bwd_local(first, carry):
        lam_re, lam_im = lam_s[0], lam_s[1]
        rows, xs = gf[pl.ds(first, 8), :], xf[pl.ds(first, 8), :]
        re, im, sum_re, sum_im = carry
        for j in reversed(order):
            re, im = lam_re * re - lam_im * im + rows[j : j + 1, :], lam_re * im + lam_im * re
            sum_re = sum_re + xs[j : j + 1, :] * re
            sum_im = sum_im + xs[j : j + 1, :] * im
        return re, im, sum_re, sum_im

    re, im, sum_re, sum_im = sweep((zero, zero, zero, zero), bwd_local, True)
    put_pieces(e_buf.at[pl.ds(GROUP, GROUP)], (re, im))
    scatter(e_buf.at[pl.ds(GROUP, GROUP)], r1b, 4)
    lam = lam_s[0], lam_s[1]
    extra = cmul(cmul(lam, (re, im)), get_pieces(hin))
    read_re = gain * sum_re + extra[0]
    read_im = -(gain * sum_im + extra[1])
    skip_part = jnp.sum(gf[...] * xf[...], axis=0, keepdims=True)
    gb[...] = jnp.zeros_like(gb)
    for half_id in range(2):
        cols = slice(128 * half_id, 128 * half_id + 128)
        for o in range(OWNERS):
            rows = (read_re if o < 16 else read_im)[2 * (o % 16) : 2 * (o % 16) + 2, cols]
            gb[half_id, o, 0:2, :] = rows
        gb[half_id, 0, 2:3, :] = skip_part[:, cols]
    copy(gb.at[1 - c], ra1g, 5, other).start()
    sends.append((gb.at[0], 5))
    arrive(ra1p, 3)
    for o in range(OWNERS):
        a2s[o, 0:2] = pb[c, o] + ra1p[o]
    ra2[me, 0:2] = a2s[me, 0:2]
    for k in range(1, OWNERS):
        o, device = owner(k)
        copy(a2s.at[o, pl.ds(0, 2)], ra2.at[me, pl.ds(0, 2)], 6, device).start()
    sends.append((ra1p.at[pl.ds(0, OWNERS - 1)], 6))
    arrive(ra1g, 5)
    for o in range(OWNERS):
        a2s[o, 2] = gb[c, o] + ra1g[o]
    ra2[me, 2] = a2s[me, 2]
    for k in range(1, OWNERS):
        o, device = owner(k)
        copy(a2s.at[o, 2], ra2.at[me, 2], 12, device).start()
    sends.append((ra1g.at[pl.ds(0, OWNERS - 1)], 12))

    arrive(r1b.at[seven], 4)
    t = block_total(r1b, down)
    t_buf[1, 0:8, :], t_buf[1, 8:16, :] = t
    spread(t_buf.at[1], r2b, 7)

    out_ref[...] = (
        xf[...] + jnp.dot(hidden, proj_ref[...], preferred_element_type=F32)
    ).astype(jnp.bfloat16)

    def bwd_read(first, carry):
        lam_re, lam_im = lam_s[0], lam_s[1]
        cof_re, cof_im = cof_s[0], cof_s[1]
        rows = gf[pl.ds(first, 8), :]
        re, im = carry
        acc = jnp.zeros((8, CHANNELS), F32)
        for j in reversed(order):
            re, im = lam_re * re - lam_im * im + rows[j : j + 1, :], lam_re * im + lam_im * re
            total = jnp.sum(cof_re * re - cof_im * im, axis=0, keepdims=True)
            acc = jnp.where(row_id == j, total, acc)
        il[pl.ds(first, 8), :] = acc + rows * skip_ref[...]
        return re, im

    sweep((zero, zero), bwd_read, True)
    il[...] = il[...] + cot_ref[...].astype(F32)

    arrive(ra2.at[pl.ds(0, OWNERS - 1), pl.ds(0, 2)], 6)
    arrive(ra2.at[pl.ds(0, OWNERS - 1), 2], 12)
    total = ra2[0]
    for o in range(1, OWNERS):
        total = total + ra2[o]
    pc[0] = total
    spread(pc.at[0], ra3, 8)

    arrive(r2b.at[seven], 7)
    entering(r1b, r2b, o_buf.at[1], down, True)
    scatter(o_buf.at[1], lin, 9)

    arrive(ra3.at[seven], 8)
    total = ra3[0]
    for o in range(1, BLOCKS):
        total = total + ra3[o]
    full[c, me] = total
    for k in range(1, OWNERS):
        copy(full.at[c, me], full.at[c, me], 10, owner(k)[1]).start()
    sends.append((ra2.at[pl.ds(0, OWNERS - 1)], 10))

    arrive(lin.at[seven], 9)
    carried = cmul((cof_s[0], cof_s[1]), get_pieces(lin))

    def bwd_inject(first, carry):
        lam_re, lam_im = lam_s[0], lam_s[1]
        re, im = carry
        acc = jnp.zeros((8, CHANNELS), F32)
        for j in reversed(order):
            re, im = lam_re * re - lam_im * im, lam_re * im + lam_im * re
            acc = jnp.where(row_id == j, jnp.sum(re, axis=0, keepdims=True), acc)
        il[pl.ds(first, 8), :] = il[pl.ds(first, 8), :] + acc
        return re, im

    sweep(carried, bwd_inject, True)
    ig_ref[...] = il[...].astype(jnp.bfloat16)

    arrive(full.at[c, pl.ds(0, OWNERS - 1)], 10)
    copy(full.at[c], full.at[c], 11, other).start()
    sends.append((full.at[0], 11))
    arrive(full.at[1 - c], 11)
    for ref, n in sends:
        copy(ref, ref, n, other).wait_send()


def finish(
    out_ref, ig_ref, full,
    out_hbm, ig_hbm, pg_hbm, rg_hbm, sg_hbm,
    pg_ref, rg_ref, sg_ref, sem,
):
    def write(src, dst, i):
        done = pltpu.make_async_copy(src, dst, sem.at[i])
        done.start()
        return done

    writes = [write(out_ref, out_hbm, 0), write(ig_ref, ig_hbm, 1)]
    squares = jnp.zeros((3, 4, 128), F32)
    for half_id in range(2):
        for o in range(OWNERS):
            v = full[half_id, o]
            squares = squares + v * v
    squares = squares[0] + squares[1] + squares[2]
    norm = jnp.sqrt(jnp.sum(jnp.sum(squares, axis=0, keepdims=True), axis=1, keepdims=True))
    factor = jnp.minimum(1.0, CEILING / (norm + 1e-06))
    for half_id in range(2):
        cols = slice(128 * half_id, 128 * half_id + 128)
        for o in range(OWNERS):
            for q in range(2):
                row = 8 * o + 4 * q
                pg_ref[row : row + 4, cols] = full[half_id, o, q] * factor
            row = 2 * (o % 16)
            rg_ref[o // 16, row : row + 2, cols] = full[half_id, o, 2, 0:2, :] * factor
        sg_ref[:, cols] = full[half_id, 0, 2, 2:3, :] * factor
    writes += [write(pg_ref, pg_hbm, 2), write(rg_ref, rg_hbm, 3), write(sg_ref, sg_hbm, 4)]
    for done in writes:
        done.wait()


def shards(inputs, cotangent, decay_rate, rotation, readout, skip_gain, projection):
    bf16 = jnp.bfloat16
    row, state, square = (RUN, CHANNELS), (2, STATES, CHANNELS), (CHANNELS, CHANNELS)
    pieces = (GROUP, 16, 128)
    sums = (2, OWNERS, 3, 4, 128)
    vmem = pl.BlockSpec(memory_space=pltpu.VMEM)
    hbm = pl.BlockSpec(memory_space=pltpu.HBM)
    operands = [
        pltpu.VMEM(row, bf16), pltpu.VMEM(row, bf16), pltpu.VMEM(state[1:], F32),
        pltpu.VMEM(state[1:], F32), pltpu.VMEM(state, F32), pltpu.VMEM((1, CHANNELS), F32),
        pltpu.VMEM(square, bf16),
    ]
    shapes = [row] * 5 + [state, state, pieces, pieces]
    shapes += [(2 * GROUP, 16, 128), (2,) + pieces, (2, 16, 128)] + [pieces] * 6
    shapes += [(2, OWNERS, 2, 4, 128), (2, OWNERS, 4, 128), (OWNERS, 2, 4, 128), (OWNERS, 4, 128)]
    shapes += [sums[1:], sums[1:], (1, 3, 4, 128), (BLOCKS, 3, 4, 128)]
    out, in_grad, total = pl.pallas_call(
        kernel,
        out_shape=(
            jax.ShapeDtypeStruct(row, bf16),
            jax.ShapeDtypeStruct(row, bf16),
            jax.ShapeDtypeStruct(sums, F32),
        ),
        in_specs=[hbm] * 7,
        out_specs=[vmem] * 3,
        scratch_shapes=operands
        + [pltpu.VMEM(shape, F32) for shape in shapes]
        + [pltpu.SemaphoreType.DMA((7,)), pltpu.SemaphoreType.DMA((13,)), pltpu.SemaphoreType.DMA((13,))],
        compiler_params=pltpu.CompilerParams(
            collective_id=0, has_side_effects=True, vmem_limit_bytes=32 << 20
        ),
        name="layer",
    )(
        *(
            pltpu.with_memory_space_constraint(v, pltpu.HBM)
            for v in (
                inputs[0], cotangent[0], decay_rate, rotation, readout,
                skip_gain.reshape(1, CHANNELS), projection,
            )
        )
    )
    outs = pl.pallas_call(
        finish,
        out_shape=(
            jax.ShapeDtypeStruct(row, bf16),
            jax.ShapeDtypeStruct(row, bf16),
            jax.ShapeDtypeStruct(square, F32),
            jax.ShapeDtypeStruct(state, F32),
            jax.ShapeDtypeStruct((1, CHANNELS), F32),
        ),
        in_specs=[vmem] * 3,
        out_specs=[hbm] * 5,
        scratch_shapes=[
            pltpu.VMEM(square, F32), pltpu.VMEM(state, F32), pltpu.VMEM((1, CHANNELS), F32),
            pltpu.SemaphoreType.DMA((5,)),
        ],
        compiler_params=pltpu.CompilerParams(vmem_limit_bytes=4 << 20),
        name="finish",
    )(out, in_grad, total)
    return outs[0][None], outs[1][None], outs[2], outs[3], outs[4].reshape(CHANNELS)


def solution(mesh):
    split = P("batch", "seq", None)
    return jax.shard_map(
        shards,
        mesh=mesh,
        in_specs=(split, split, P(), P(), P(), P(), P()),
        out_specs=(split, split, P(), P(), P()),
        check_vma=False,
    )
```

```python
import math

import jax
import jax.numpy as jnp
import numpy as np
from jax import lax
from jax.experimental import pallas as pl
from jax.experimental.pallas import tpu as pltpu
from jax.sharding import PartitionSpec as P

MESH = pl.DeviceIdType.MESH
F32 = jnp.float32
STATES, CHANNELS, RUN = 32, 256, 128
GROUP = 8
BLOCKS = 8
OWNERS = 32

TURN_HI = 6.28125
TURN_MID = round((2 * math.pi - TURN_HI) * 2**20) / 2**20
TURN_LO = 2 * math.pi - TURN_HI - TURN_MID
GELU_SCALE = math.sqrt(2 / math.pi)
GELU_CUBE = 0.044715
CEILING = math.sqrt(CHANNELS * CHANNELS + 2 * STATES * CHANNELS + CHANNELS)


def cmul(a, b):
    return a[0] * b[0] - a[1] * b[1], a[0] * b[1] + a[1] * b[0]


def decay_power(decay, rotation, times):
    angle = rotation * float(times)
    if times > 1:
        turns = jnp.floor(angle * (0.5 / math.pi) + 0.5)
        angle = ((angle - turns * TURN_HI) - turns * TURN_MID) - turns * TURN_LO
    size = jnp.exp(decay * -float(times))
    return size * jnp.cos(angle), size * jnp.sin(angle)


def entry_gain(decay):
    y = 2.0 * decay
    series = 1.0 - y * (1.0 / 8)
    for k in (7, 6, 5, 4, 3, 2):
        series = 1.0 - y * (1.0 / k) * series
    return jnp.sqrt(jnp.where(y < 0.25, y * series, 1.0 - jnp.exp(-y)))


def put_pieces(ref, value):
    re, im = value
    for p in range(GROUP):
        rows, cols = slice(8 * (p // 2), 8 * (p // 2) + 8), slice(128 * (p % 2), 128 * (p % 2) + 128)
        ref[p, 0:8, :] = re[rows, cols]
        ref[p, 8:16, :] = im[rows, cols]


def get_pieces(ref):
    def part(lo):
        return jnp.concatenate(
            [
                jnp.concatenate([ref[2 * n, lo : lo + 8, :], ref[2 * n + 1, lo : lo + 8, :]], axis=1)
                for n in range(4)
            ],
            axis=0,
        )

    return part(0), part(8)


def load(ref, i):
    return ref[i, 0:8, :], ref[i, 8:16, :]


def store(ref, i, value):
    ref[i, 0:8, :] = value[0]
    ref[i, 8:16, :] = value[1]


def kernel(
    x_hbm, cot_hbm, decay_hbm, rot_hbm, read_hbm, skip_hbm, proj_hbm,
    out_ref, ig_ref, full,
    x_ref, cot_ref, decay_ref, rot_ref, read_ref, skip_ref, proj_ref,
    xf, gf, mix, hb, il,
    lam_s, cof_s, l128, l1024,
    e_buf, o_buf, t_buf, r1f, r2f, hin, r1b, r2b, lin,
    pb, gb, ra1p, ra1g, a2s, ra2, pc, ra3,
    isem, ssem, rsem, near_sem, far_sem,
):
    s, b = lax.axis_index("seq"), lax.axis_index("batch")
    g, blk = lax.rem(s, GROUP), lax.div(s, GROUP)
    y, c = lax.div(b, 2), lax.rem(b, 2)
    me = lax.div(g, 4) * 16 + lax.rem(g, 4) * 4 + y

    base = blk * GROUP
    zs = [lax.rem(lax.div(g, 4) + k, 2) for k in range(2)]
    xs = [lax.rem(lax.rem(g, 4) + k, 4) for k in range(4)]
    ys = [lax.rem(y + k, 4) for k in range(4)]
    seqs = [[base + z * 4 + x for x in xs] for z in zs]
    batches = [v * 2 + c for v in ys]
    in_block = [
        (zs[k // 4] * 4 + xs[k % 4], {"seq": seqs[k // 4][k % 4], "batch": b})
        for k in range(1, GROUP)
    ]
    across = [{"seq": lax.rem(blk + k, BLOCKS) * GROUP + g, "batch": b} for k in range(BLOCKS)]
    owners = [
        (
            zs[k // 16] * 16 + xs[k // 4 % 4] * 4 + ys[k % 4],
            {"seq": seqs[k // 16][k // 4 % 4], "batch": batches[k % 4]},
        )
        for k in range(1, OWNERS)
    ]
    other = {"seq": s, "batch": y * 2 + (1 - c)}

    fetches = [
        pltpu.make_async_copy(src, dst, isem.at[i])
        for i, (src, dst) in enumerate(
            [(decay_hbm, decay_ref), (rot_hbm, rot_ref), (read_hbm, read_ref), (x_hbm, x_ref),
             (skip_hbm, skip_ref), (cot_hbm, cot_ref), (proj_hbm, proj_ref)]
        )
    ]
    for fetch in fetches:
        fetch.start()

    barrier = pltpu.get_barrier_semaphore()
    partners = [device for _, device in in_block] + [across[1], across[7], other]
    partners += [{"seq": s, "batch": batch} for batch in batches[1:]]

    def greet(sem, devices):
        for device in devices:
            pl.semaphore_signal(sem, inc=1, device_id=device, device_id_type=MESH)

    greet(barrier, partners)

    def copy(src, dst, n, device):
        return pltpu.make_async_remote_copy(
            src_ref=src, dst_ref=dst, send_sem=ssem.at[n], recv_sem=rsem.at[n],
            device_id=device, device_id_type=MESH,
        )

    for fetch in fetches:
        fetch.wait()

    decay, rot = decay_ref[...], rot_ref[...]
    gain = entry_gain(decay)
    lam = decay_power(decay, rot, 1)
    put_pieces(l128, decay_power(decay, rot, RUN))
    put_pieces(l1024, decay_power(decay, rot, RUN * GROUP))
    lam_s[0], lam_s[1] = lam
    cof_s[0] = gain * read_ref[0]
    cof_s[1] = gain * read_ref[1]
    xf[...] = x_ref[...].astype(F32)
    row_id = lax.broadcasted_iota(jnp.int32, (8, CHANNELS), 0)
    zero = jnp.zeros((STATES, CHANNELS), F32)

    def sweep(carry, body, backward=False, lo=0, hi=RUN // 8):
        def step(i, carry):
            first = RUN - 8 - 8 * i if backward else 8 * i
            return body(pl.multiple_of(first, 8), carry)

        return lax.fori_loop(lo, hi, step, carry)

    order = tuple(range(8))

    def fwd_state(first, carry):
        lam_re, lam_im = lam_s[0], lam_s[1]
        rows = xf[pl.ds(first, 8), :]
        re, im = carry
        for j in order:
            re, im = lam_re * re - lam_im * im + rows[j : j + 1, :], lam_re * im + lam_im * re
        return re, im

    def fwd_local(first, carry):
        lam_re, lam_im = lam_s[0], lam_s[1]
        cof_re, cof_im = cof_s[0], cof_s[1]
        rows = xf[pl.ds(first, 8), :]
        re, im = carry
        acc = jnp.zeros((8, CHANNELS), F32)
        for j in order:
            re, im = lam_re * re - lam_im * im + rows[j : j + 1, :], lam_re * im + lam_im * re
            total = jnp.sum(cof_re * re - cof_im * im, axis=0, keepdims=True)
            acc = jnp.where(row_id == j, total, acc)
        mix[pl.ds(first, 8), :] = acc + rows * skip_ref[...]
        return re, im

    re, im = sweep((zero, zero), fwd_state)
    put_pieces(e_buf, (gain * re, gain * im))
    pl.semaphore_wait(barrier, len(partners))

    sends = []

    def scatter(buf, dst, n):
        dst[g] = buf[g]
        for p, device in in_block:
            copy(buf.at[p], dst.at[g], n, device).start()
        sends.append((buf.at[pl.ds(0, GROUP - 1)], n))

    def spread(src, dst, n):
        dst[blk] = src[...]
        for k in (4, 5, 3, 6, 2, 7, 1):
            copy(src, dst.at[blk], n, across[k]).start()
        sends.append((dst.at[pl.ds(0, BLOCKS - 1)], n))

    def arrive(ref, n):
        copy(ref, ref, n, other).wait_recv()

    def block_total(r1, turn):
        step = load(l128, g)
        total = load(r1, turn[0])
        for i in turn[1:]:
            moved = cmul(step, total)
            nxt = load(r1, i)
            total = moved[0] + nxt[0], moved[1] + nxt[1]
        return total

    def entering(r1, r2, buf, turn, backward):
        step, leap = load(l128, g), load(l1024, g)
        state = (jnp.zeros((8, 128), F32), jnp.zeros((8, 128), F32))
        for i in turn:
            moved, nxt = cmul(leap, state), load(r2, i)
            use = (i > blk) if backward else (i < blk)
            state = tuple(jnp.where(use, m + v, old) for m, v, old in zip(moved, nxt, state))
        for i in turn:
            store(buf, i, state)
            moved, nxt = cmul(step, state), load(r1, i)
            state = moved[0] + nxt[0], moved[1] + nxt[1]

    up, down = tuple(range(8)), tuple(range(7, -1, -1))
    seven = pl.ds(0, 7)

    scatter(e_buf, r1f, 0)
    greet(near_sem, (across[1], across[7]))
    state = sweep((zero, zero), fwd_local, hi=RUN // 16)
    pl.semaphore_wait(near_sem, 2)
    greet(far_sem, (across[2], across[6]))
    sweep(state, fwd_local, lo=RUN // 16)
    hb[...] = lax.dot_general(
        cot_ref[...], proj_ref[...], (((1,), (1,)), ((), ())), preferred_element_type=F32
    )
    pl.semaphore_wait(far_sem, 2)
    arrive(r1f.at[seven], 0)
    t = block_total(r1f, up)
    t_buf[0, 0:8, :], t_buf[0, 8:16, :] = t
    spread(t_buf.at[0], r2f, 1)
    arrive(r2f.at[seven], 1)
    entering(r1f, r2f, o_buf.at[0], up, False)
    scatter(o_buf.at[0], hin, 2)
    arrive(hin.at[seven], 2)

    enter = get_pieces(hin)
    carried = cmul((read_ref[0], read_ref[1]), enter)

    def fwd_inject(first, carry):
        lam_re, lam_im = lam_s[0], lam_s[1]
        re, im = carry
        acc = jnp.zeros((8, CHANNELS), F32)
        for j in order:
            re, im = lam_re * re - lam_im * im, lam_re * im + lam_im * re
            acc = jnp.where(row_id == j, jnp.sum(re, axis=0, keepdims=True), acc)
        mix[pl.ds(first, 8), :] = mix[pl.ds(first, 8), :] + acc
        return re, im

    sweep(carried, fwd_inject)

    mixed = mix[...]
    square = mixed * mixed
    tanh = jnp.tanh(GELU_SCALE * (mixed + GELU_CUBE * (mixed * square)))
    half = 0.5 * (1.0 + tanh)
    hidden = (mixed * half).astype(jnp.bfloat16)
    slope = half + (0.5 * mixed) * (1.0 - tanh * tanh) * (
        GELU_SCALE * (1.0 + (3.0 * GELU_CUBE) * square)
    )
    grad = hb[...] * slope
    gf[...] = grad
    part = lax.dot_general(
        hidden, cot_ref[...], (((0,), (0,)), ((), ())), preferred_element_type=F32
    )
    for half_id in range(2):
        for o in range(OWNERS):
            for q in range(2):
                row = 8 * o + 4 * q
                pb[half_id, o, q] = part[row : row + 4, 128 * half_id : 128 * half_id + 128]
    copy(pb.at[1 - c], ra1p, 3, other).start()
    sends.append((pb.at[0], 3))

    def bwd_local(first, carry):
        lam_re, lam_im = lam_s[0], lam_s[1]
        rows, xs = gf[pl.ds(first, 8), :], xf[pl.ds(first, 8), :]
        re, im, sum_re, sum_im = carry
        for j in reversed(order):
            re, im = lam_re * re - lam_im * im + rows[j : j + 1, :], lam_re * im + lam_im * re
            sum_re = sum_re + xs[j : j + 1, :] * re
            sum_im = sum_im + xs[j : j + 1, :] * im
        return re, im, sum_re, sum_im

    re, im, sum_re, sum_im = sweep((zero, zero, zero, zero), bwd_local, True)
    put_pieces(e_buf.at[pl.ds(GROUP, GROUP)], (re, im))
    scatter(e_buf.at[pl.ds(GROUP, GROUP)], r1b, 4)
    lam = lam_s[0], lam_s[1]
    extra = cmul(cmul(lam, (re, im)), get_pieces(hin))
    read_re = gain * sum_re + extra[0]
    read_im = -(gain * sum_im + extra[1])
    skip_part = jnp.sum(gf[...] * xf[...], axis=0, keepdims=True)
    gb[...] = jnp.zeros_like(gb)
    for half_id in range(2):
        cols = slice(128 * half_id, 128 * half_id + 128)
        for o in range(OWNERS):
            rows = (read_re if o < 16 else read_im)[2 * (o % 16) : 2 * (o % 16) + 2, cols]
            gb[half_id, o, 0:2, :] = rows
        gb[half_id, 0, 2:3, :] = skip_part[:, cols]
    copy(gb.at[1 - c], ra1g, 5, other).start()
    sends.append((gb.at[0], 5))
    arrive(ra1p, 3)
    for o in range(OWNERS):
        a2s[o, 0:2] = pb[c, o] + ra1p[o]
    arrive(ra1g, 5)
    for o in range(OWNERS):
        a2s[o, 2] = gb[c, o] + ra1g[o]
    ra2[me] = a2s[me]
    for o, device in owners:
        copy(a2s.at[o], ra2.at[me], 6, device).start()
    sends.append((ra2.at[pl.ds(0, OWNERS - 1)], 6))

    arrive(r1b.at[seven], 4)
    t = block_total(r1b, down)
    t_buf[1, 0:8, :], t_buf[1, 8:16, :] = t
    spread(t_buf.at[1], r2b, 7)


    arrive(ra2.at[pl.ds(0, OWNERS - 1)], 6)
    total = ra2[0]
    for o in range(1, OWNERS):
        total = total + ra2[o]
    pc[0] = total
    spread(pc.at[0], ra3, 8)

    out_ref[...] = (
        xf[...] + jnp.dot(hidden, proj_ref[...], preferred_element_type=F32)
    ).astype(jnp.bfloat16)

    def bwd_read(first, carry):
        lam_re, lam_im = lam_s[0], lam_s[1]
        cof_re, cof_im = cof_s[0], cof_s[1]
        rows = gf[pl.ds(first, 8), :]
        re, im = carry
        acc = jnp.zeros((8, CHANNELS), F32)
        for j in reversed(order):
            re, im = lam_re * re - lam_im * im + rows[j : j + 1, :], lam_re * im + lam_im * re
            total = jnp.sum(cof_re * re - cof_im * im, axis=0, keepdims=True)
            acc = jnp.where(row_id == j, total, acc)
        il[pl.ds(first, 8), :] = acc + rows * skip_ref[...]
        return re, im

    sweep((zero, zero), bwd_read, True)
    il[...] = il[...] + cot_ref[...].astype(F32)

    arrive(r2b.at[seven], 7)
    entering(r1b, r2b, o_buf.at[1], down, True)
    scatter(o_buf.at[1], lin, 9)

    arrive(ra3.at[seven], 8)
    total = ra3[0]
    for o in range(1, BLOCKS):
        total = total + ra3[o]
    full[c, me] = total
    for _, device in owners:
        copy(full.at[c, me], full.at[c, me], 10, device).start()
    sends.append((ra2.at[pl.ds(0, OWNERS - 1)], 10))

    arrive(lin.at[seven], 9)
    carried = cmul((cof_s[0], cof_s[1]), get_pieces(lin))

    def bwd_inject(first, carry):
        lam_re, lam_im = lam_s[0], lam_s[1]
        re, im = carry
        acc = jnp.zeros((8, CHANNELS), F32)
        for j in reversed(order):
            re, im = lam_re * re - lam_im * im, lam_re * im + lam_im * re
            acc = jnp.where(row_id == j, jnp.sum(re, axis=0, keepdims=True), acc)
        il[pl.ds(first, 8), :] = il[pl.ds(first, 8), :] + acc
        return re, im

    sweep(carried, bwd_inject, True)
    ig_ref[...] = il[...].astype(jnp.bfloat16)

    arrive(full.at[c, pl.ds(0, OWNERS - 1)], 10)
    copy(full.at[c], full.at[c], 11, other).start()
    sends.append((full.at[0], 11))
    arrive(full.at[1 - c], 11)
    for ref, n in sends:
        copy(ref, ref, n, other).wait_send()


def finish(
    out_ref, ig_ref, full,
    out_hbm, ig_hbm, pg_hbm, rg_hbm, sg_hbm,
    pg_ref, rg_ref, sg_ref, sem,
):
    def write(src, dst, i):
        done = pltpu.make_async_copy(src, dst, sem.at[i])
        done.start()
        return done

    writes = [write(out_ref, out_hbm, 0), write(ig_ref, ig_hbm, 1)]
    squares = jnp.zeros((3, 4, 128), F32)
    for half_id in range(2):
        for o in range(OWNERS):
            v = full[half_id, o]
            squares = squares + v * v
    squares = squares[0] + squares[1] + squares[2]
    norm = jnp.sqrt(jnp.sum(jnp.sum(squares, axis=0, keepdims=True), axis=1, keepdims=True))
    factor = jnp.minimum(1.0, CEILING / (norm + 1e-06))
    for half_id in range(2):
        cols = slice(128 * half_id, 128 * half_id + 128)
        for o in range(OWNERS):
            for q in range(2):
                row = 8 * o + 4 * q
                pg_ref[row : row + 4, cols] = full[half_id, o, q] * factor
            row = 2 * (o % 16)
            rg_ref[o // 16, row : row + 2, cols] = full[half_id, o, 2, 0:2, :] * factor
        sg_ref[:, cols] = full[half_id, 0, 2, 2:3, :] * factor
    writes += [write(pg_ref, pg_hbm, 2), write(rg_ref, rg_hbm, 3), write(sg_ref, sg_hbm, 4)]
    for done in writes:
        done.wait()


def shards(inputs, cotangent, decay_rate, rotation, readout, skip_gain, projection):
    bf16 = jnp.bfloat16
    row, state, square = (RUN, CHANNELS), (2, STATES, CHANNELS), (CHANNELS, CHANNELS)
    pieces = (GROUP, 16, 128)
    sums = (2, OWNERS, 3, 4, 128)
    vmem = pl.BlockSpec(memory_space=pltpu.VMEM)
    hbm = pl.BlockSpec(memory_space=pltpu.HBM)
    operands = [
        pltpu.VMEM(row, bf16), pltpu.VMEM(row, bf16), pltpu.VMEM(state[1:], F32),
        pltpu.VMEM(state[1:], F32), pltpu.VMEM(state, F32), pltpu.VMEM((1, CHANNELS), F32),
        pltpu.VMEM(square, bf16),
    ]
    shapes = [row] * 5 + [state, state, pieces, pieces]
    shapes += [(2 * GROUP, 16, 128), (2,) + pieces, (2, 16, 128)] + [pieces] * 6
    shapes += [(2, OWNERS, 2, 4, 128), (2, OWNERS, 4, 128), (OWNERS, 2, 4, 128), (OWNERS, 4, 128)]
    shapes += [sums[1:], sums[1:], (1, 3, 4, 128), (BLOCKS, 3, 4, 128)]
    out, in_grad, total = pl.pallas_call(
        kernel,
        out_shape=(
            jax.ShapeDtypeStruct(row, bf16),
            jax.ShapeDtypeStruct(row, bf16),
            jax.ShapeDtypeStruct(sums, F32),
        ),
        in_specs=[hbm] * 7,
        out_specs=[vmem] * 3,
        scratch_shapes=operands
        + [pltpu.VMEM(shape, F32) for shape in shapes]
        + [pltpu.SemaphoreType.DMA((7,)), pltpu.SemaphoreType.DMA((12,)), pltpu.SemaphoreType.DMA((12,)), pltpu.SemaphoreType.REGULAR, pltpu.SemaphoreType.REGULAR],
        compiler_params=pltpu.CompilerParams(
            collective_id=0, has_side_effects=True, vmem_limit_bytes=32 << 20
        ),
        name="layer",
    )(
        *(
            pltpu.with_memory_space_constraint(v, pltpu.HBM)
            for v in (
                inputs[0], cotangent[0], decay_rate, rotation, readout,
                skip_gain.reshape(1, CHANNELS), projection,
            )
        )
    )
    outs = pl.pallas_call(
        finish,
        out_shape=(
            jax.ShapeDtypeStruct(row, bf16),
            jax.ShapeDtypeStruct(row, bf16),
            jax.ShapeDtypeStruct(square, F32),
            jax.ShapeDtypeStruct(state, F32),
            jax.ShapeDtypeStruct((1, CHANNELS), F32),
        ),
        in_specs=[vmem] * 3,
        out_specs=[hbm] * 5,
        scratch_shapes=[
            pltpu.VMEM(square, F32), pltpu.VMEM(state, F32), pltpu.VMEM((1, CHANNELS), F32),
            pltpu.SemaphoreType.DMA((5,)),
        ],
        compiler_params=pltpu.CompilerParams(vmem_limit_bytes=4 << 20),
        name="finish",
    )(out, in_grad, total)
    return outs[0][None], outs[1][None], outs[2], outs[3], outs[4].reshape(CHANNELS)


def solution(mesh):
    split = P("batch", "seq", None)
    return jax.shard_map(
        shards,
        mesh=mesh,
        in_specs=(split, split, P(), P(), P(), P(), P()),
        out_specs=(split, split, P(), P(), P()),
        check_vma=False,
    )
```

```python
import math

import jax
import jax.numpy as jnp
import numpy as np
from jax import lax
from jax.experimental import pallas as pl
from jax.experimental.pallas import tpu as pltpu
from jax.sharding import PartitionSpec as P

MESH = pl.DeviceIdType.MESH
F32 = jnp.float32
STATES, CHANNELS, RUN = 32, 256, 128
GROUP = 8
BLOCKS = 8
OWNERS = 32

TURN_HI = 6.28125
TURN_MID = round((2 * math.pi - TURN_HI) * 2**20) / 2**20
TURN_LO = 2 * math.pi - TURN_HI - TURN_MID
GELU_SCALE = math.sqrt(2 / math.pi)
GELU_CUBE = 0.044715
CEILING = math.sqrt(CHANNELS * CHANNELS + 2 * STATES * CHANNELS + CHANNELS)


def cmul(a, b):
    return a[0] * b[0] - a[1] * b[1], a[0] * b[1] + a[1] * b[0]


def decay_power(decay, rotation, times):
    angle = rotation * float(times)
    if times > 1:
        turns = jnp.floor(angle * (0.5 / math.pi) + 0.5)
        angle = ((angle - turns * TURN_HI) - turns * TURN_MID) - turns * TURN_LO
    size = jnp.exp(decay * -float(times))
    return size * jnp.cos(angle), size * jnp.sin(angle)


def entry_gain(decay):
    y = 2.0 * decay
    series = 1.0 - y * (1.0 / 8)
    for k in (7, 6, 5, 4, 3, 2):
        series = 1.0 - y * (1.0 / k) * series
    return jnp.sqrt(jnp.where(y < 0.25, y * series, 1.0 - jnp.exp(-y)))


def put_pieces(ref, value):
    re, im = value
    for p in range(GROUP):
        rows, cols = slice(8 * (p // 2), 8 * (p // 2) + 8), slice(128 * (p % 2), 128 * (p % 2) + 128)
        ref[p, 0:8, :] = re[rows, cols]
        ref[p, 8:16, :] = im[rows, cols]


def get_pieces(ref):
    def part(lo):
        return jnp.concatenate(
            [
                jnp.concatenate([ref[2 * n, lo : lo + 8, :], ref[2 * n + 1, lo : lo + 8, :]], axis=1)
                for n in range(4)
            ],
            axis=0,
        )

    return part(0), part(8)


def load(ref, i):
    return ref[i, 0:8, :], ref[i, 8:16, :]


def store(ref, i, value):
    ref[i, 0:8, :] = value[0]
    ref[i, 8:16, :] = value[1]


def kernel(
    x_hbm, cot_hbm, decay_hbm, rot_hbm, read_hbm, skip_hbm, proj_hbm,
    out_ref, ig_ref, full,
    x_ref, cot_ref, decay_ref, rot_ref, read_ref, skip_ref, proj_ref,
    xf, gf, mix, hb, il,
    tab, lam_s, cof_s, l128, l1024,
    e_buf, o_buf, t_buf, r1f, r2f, hin, r1b, r2b, lin,
    pb, gb, ra1p, ra1g, a2s, ra2, pc, ra3,
    isem, ssem, rsem, far_sem,
):
    s, b = lax.axis_index("seq"), lax.axis_index("batch")
    g, blk = lax.rem(s, GROUP), lax.div(s, GROUP)
    y, c = lax.div(b, 2), lax.rem(b, 2)
    me = lax.div(g, 4) * 16 + lax.rem(g, 4) * 4 + y

    base = blk * GROUP
    zs = [lax.rem(lax.div(g, 4) + k, 2) for k in range(2)]
    xs = [lax.rem(lax.rem(g, 4) + k, 4) for k in range(4)]
    ys = [lax.rem(y + k, 4) for k in range(4)]
    seqs = [[base + z * 4 + x for x in xs] for z in zs]
    batches = [v * 2 + c for v in ys]
    in_block = [
        (zs[k // 4] * 4 + xs[k % 4], {"seq": seqs[k // 4][k % 4], "batch": b})
        for k in range(1, GROUP)
    ]
    across = [{"seq": lax.rem(blk + k, BLOCKS) * GROUP + g, "batch": b} for k in range(BLOCKS)]
    owners = [
        (
            zs[k // 16] * 16 + xs[k // 4 % 4] * 4 + ys[k % 4],
            {"seq": seqs[k // 16][k // 4 % 4], "batch": batches[k % 4]},
        )
        for k in range(1, OWNERS)
    ]
    other = {"seq": s, "batch": y * 2 + (1 - c)}

    fetches = [
        pltpu.make_async_copy(src, dst, isem.at[i])
        for i, (src, dst) in enumerate(
            [(decay_hbm, decay_ref), (rot_hbm, rot_ref), (read_hbm, read_ref), (x_hbm, x_ref),
             (skip_hbm, skip_ref), (cot_hbm, cot_ref), (proj_hbm, proj_ref)]
        )
    ]
    for fetch in fetches:
        fetch.start()

    barrier = pltpu.get_barrier_semaphore()
    partners = [device for _, device in in_block] + [across[k] for k in (1, 2, 6, 7)] + [other]
    partners += [{"seq": s, "batch": batch} for batch in batches[1:]]

    def greet(sem, devices):
        for device in devices:
            pl.semaphore_signal(sem, inc=1, device_id=device, device_id_type=MESH)

    greet(barrier, partners)

    def copy(src, dst, n, device):
        return pltpu.make_async_remote_copy(
            src_ref=src, dst_ref=dst, send_sem=ssem.at[n], recv_sem=rsem.at[n],
            device_id=device, device_id_type=MESH,
        )

    for fetch in fetches:
        fetch.wait()

    decay, rot = decay_ref[...], rot_ref[...]
    gain = entry_gain(decay)
    lam = decay_power(decay, rot, 1)
    put_pieces(l128, decay_power(decay, rot, RUN))
    put_pieces(l1024, decay_power(decay, rot, RUN * GROUP))
    lam_s[0], lam_s[1] = lam
    cof_s[0] = gain * read_ref[0]
    cof_s[1] = gain * read_ref[1]
    xf[...] = x_ref[...].astype(F32)
    row_id = lax.broadcasted_iota(jnp.int32, (8, CHANNELS), 0)
    zero = jnp.zeros((STATES, CHANNELS), F32)

    def sweep(carry, body, backward=False, lo=0, hi=RUN // 8):
        def step(i, carry):
            first = RUN - 8 - 8 * i if backward else 8 * i
            return body(pl.multiple_of(first, 8), carry)

        return lax.fori_loop(lo, hi, step, carry)

    order = tuple(range(8))

    def fwd_state(first, carry):
        lam_re, lam_im = lam_s[0], lam_s[1]
        rows = xf[pl.ds(first, 8), :]
        re, im = carry
        for j in order:
            re, im = lam_re * re - lam_im * im + rows[j : j + 1, :], lam_re * im + lam_im * re
        return re, im

    def fwd_local(first, carry):
        lam_re, lam_im = lam_s[0], lam_s[1]
        cof_re, cof_im = cof_s[0], cof_s[1]
        rows = xf[pl.ds(first, 8), :]
        re, im = carry
        acc = jnp.zeros((8, CHANNELS), F32)
        for j in order:
            re, im = lam_re * re - lam_im * im + rows[j : j + 1, :], lam_re * im + lam_im * re
            total = jnp.sum(cof_re * re - cof_im * im, axis=0, keepdims=True)
            acc = jnp.where(row_id == j, total, acc)
        mix[pl.ds(first, 8), :] = acc + rows * skip_ref[...]
        return re, im

    re, im = sweep((zero, zero), fwd_state)
    put_pieces(e_buf, (gain * re, gain * im))
    pl.semaphore_wait(barrier, len(partners))

    sends = []

    def scatter(buf, dst, n):
        dst[g] = buf[g]
        for p, device in in_block:
            copy(buf.at[p], dst.at[g], n, device).start()
        sends.append((buf.at[pl.ds(0, GROUP - 1)], n))

    def spread(src, dst, n):
        dst[blk] = src[...]
        for k in (4, 5, 3, 6, 2, 7, 1):
            copy(src, dst.at[blk], n, across[k]).start()
        sends.append((dst.at[pl.ds(0, BLOCKS - 1)], n))

    def arrive(ref, n):
        copy(ref, ref, n, other).wait_recv()

    def block_total(r1, turn):
        step = load(l128, g)
        total = load(r1, turn[0])
        for i in turn[1:]:
            moved = cmul(step, total)
            nxt = load(r1, i)
            total = moved[0] + nxt[0], moved[1] + nxt[1]
        return total

    def entering(r1, r2, buf, turn, backward):
        step, leap = load(l128, g), load(l1024, g)
        state = (jnp.zeros((8, 128), F32), jnp.zeros((8, 128), F32))
        for i in turn:
            moved, nxt = cmul(leap, state), load(r2, i)
            use = (i > blk) if backward else (i < blk)
            state = tuple(jnp.where(use, m + v, old) for m, v, old in zip(moved, nxt, state))
        for i in turn:
            store(buf, i, state)
            moved, nxt = cmul(step, state), load(r1, i)
            state = moved[0] + nxt[0], moved[1] + nxt[1]

    up, down = tuple(range(8)), tuple(range(7, -1, -1))
    seven = pl.ds(0, 7)

    greet(far_sem, (across[2], across[6]))
    scatter(e_buf, r1f, 0)
    sweep((zero, zero), fwd_local)
    hb[...] = lax.dot_general(
        cot_ref[...], proj_ref[...], (((1,), (1,)), ((), ())), preferred_element_type=F32
    )
    pl.semaphore_wait(far_sem, 2)
    arrive(r1f.at[seven], 0)
    t = block_total(r1f, up)
    t_buf[0, 0:8, :], t_buf[0, 8:16, :] = t
    spread(t_buf.at[0], r2f, 1)

    def fill_table(j, power):
        tab[j, 0], tab[j, 1] = power
        return cmul((lam_s[0], lam_s[1]), power)

    lax.fori_loop(0, 16, fill_table, (lam_s[0], lam_s[1]))
    gb[...] = jnp.zeros_like(gb)
    a2s[...] = jnp.zeros_like(a2s)
    arrive(r2f.at[seven], 1)
    entering(r1f, r2f, o_buf.at[0], up, False)
    scatter(o_buf.at[0], hin, 2)
    arrive(hin.at[seven], 2)

    enter = get_pieces(hin)
    carried = cmul((read_ref[0], read_ref[1]), enter)

    def inject(carried, ref, backward):
        def step(i, carry):
            re, im = carry
            for part in range(2):
                first = 16 * i + 8 * part
                acc = jnp.zeros((8, CHANNELS), F32)
                for j in order:
                    n = 8 * part + j
                    total = jnp.sum(tab[n, 0] * re - tab[n, 1] * im, axis=0, keepdims=True)
                    acc = jnp.where(row_id == (7 - j if backward else j), total, acc)
                first = pl.multiple_of(RUN - 8 - first if backward else first, 8)
                ref[pl.ds(first, 8), :] = ref[pl.ds(first, 8), :] + acc
            return cmul((tab[15, 0], tab[15, 1]), carry)

        lax.fori_loop(0, RUN // 16, step, carried)

    inject(carried, mix, False)

    mixed = mix[...]
    square = mixed * mixed
    tanh = jnp.tanh(GELU_SCALE * (mixed + GELU_CUBE * (mixed * square)))
    half = 0.5 * (1.0 + tanh)
    hidden = (mixed * half).astype(jnp.bfloat16)
    slope = half + (0.5 * mixed) * (1.0 - tanh * tanh) * (
        GELU_SCALE * (1.0 + (3.0 * GELU_CUBE) * square)
    )
    grad = hb[...] * slope
    gf[...] = grad
    part = lax.dot_general(
        hidden, cot_ref[...], (((0,), (0,)), ((), ())), preferred_element_type=F32
    )
    for half_id in range(2):
        for o in range(OWNERS):
            for q in range(2):
                row = 8 * o + 4 * q
                pb[half_id, o, q] = part[row : row + 4, 128 * half_id : 128 * half_id + 128]
    copy(pb.at[1 - c], ra1p, 3, other).start()
    sends.append((pb.at[0], 3))

    def bwd_local(first, carry):
        lam_re, lam_im = lam_s[0], lam_s[1]
        rows, xs = gf[pl.ds(first, 8), :], xf[pl.ds(first, 8), :]
        re, im, sum_re, sum_im = carry
        for j in reversed(order):
            re, im = lam_re * re - lam_im * im + rows[j : j + 1, :], lam_re * im + lam_im * re
            sum_re = sum_re + xs[j : j + 1, :] * re
            sum_im = sum_im + xs[j : j + 1, :] * im
        return re, im, sum_re, sum_im

    re, im, sum_re, sum_im = sweep((zero, zero, zero, zero), bwd_local, True)
    put_pieces(e_buf.at[pl.ds(GROUP, GROUP)], (re, im))
    scatter(e_buf.at[pl.ds(GROUP, GROUP)], r1b, 4)
    lam = lam_s[0], lam_s[1]
    extra = cmul(cmul(lam, (re, im)), get_pieces(hin))
    read_re = gain * sum_re + extra[0]
    read_im = -(gain * sum_im + extra[1])
    skip_part = jnp.sum(gf[...] * xf[...], axis=0, keepdims=True)
    for half_id in range(2):
        cols = slice(128 * half_id, 128 * half_id + 128)
        for o in range(16):
            gb[half_id, o] = (read_re if o < 8 else read_im)[4 * (o % 8) : 4 * (o % 8) + 4, cols]
        gb[half_id, 16, 0:1, :] = skip_part[:, cols]
    copy(gb.at[1 - c], ra1g, 5, other).start()
    sends.append((gb.at[0], 5))
    arrive(ra1p, 3)
    for o in range(OWNERS):
        a2s[o, 0:2] = pb[c, o] + ra1p[o]
    ra2[me, 0:2] = a2s[me, 0:2]
    for o, device in owners:
        copy(a2s.at[o, pl.ds(0, 2)], ra2.at[me, pl.ds(0, 2)], 6, device).start()
    sends.append((ra1p.at[pl.ds(0, OWNERS - 1)], 6))
    arrive(ra1g, 5)
    for o in range(17):
        a2s[o, 2] = gb[c, o] + ra1g[o]
    ra2[me, 2] = a2s[me, 2]
    for o, device in owners:
        copy(a2s.at[o, 2], ra2.at[me, 2], 12, device).start()
    sends.append((ra2.at[pl.ds(0, OWNERS - 1), 2], 12))

    arrive(r1b.at[seven], 4)
    t = block_total(r1b, down)
    t_buf[1, 0:8, :], t_buf[1, 8:16, :] = t
    spread(t_buf.at[1], r2b, 7)


    arrive(ra2.at[pl.ds(0, OWNERS - 1), pl.ds(0, 2)], 6)
    arrive(ra2.at[pl.ds(0, OWNERS - 1), 2], 12)
    total = ra2[0]
    for o in range(1, OWNERS):
        total = total + ra2[o]
    pc[0] = total
    spread(pc.at[0], ra3, 8)

    out_ref[...] = (
        xf[...] + jnp.dot(hidden, proj_ref[...], preferred_element_type=F32)
    ).astype(jnp.bfloat16)

    def bwd_read(first, carry):
        lam_re, lam_im = lam_s[0], lam_s[1]
        cof_re, cof_im = cof_s[0], cof_s[1]
        rows = gf[pl.ds(first, 8), :]
        re, im = carry
        acc = jnp.zeros((8, CHANNELS), F32)
        for j in reversed(order):
            re, im = lam_re * re - lam_im * im + rows[j : j + 1, :], lam_re * im + lam_im * re
            total = jnp.sum(cof_re * re - cof_im * im, axis=0, keepdims=True)
            acc = jnp.where(row_id == j, total, acc)
        il[pl.ds(first, 8), :] = acc + rows * skip_ref[...]
        return re, im

    sweep((zero, zero), bwd_read, True)
    il[...] = il[...] + cot_ref[...].astype(F32)

    arrive(r2b.at[seven], 7)
    entering(r1b, r2b, o_buf.at[1], down, True)
    scatter(o_buf.at[1], lin, 9)

    arrive(ra3.at[seven], 8)
    total = ra3[0]
    for o in range(1, BLOCKS):
        total = total + ra3[o]
    full[c, me] = total
    for _, device in owners:
        copy(full.at[c, me], full.at[c, me], 10, device).start()
    sends.append((ra2.at[pl.ds(0, OWNERS - 1)], 10))

    arrive(lin.at[seven], 9)
    carried = cmul((cof_s[0], cof_s[1]), get_pieces(lin))

    inject(carried, il, True)
    ig_ref[...] = il[...].astype(jnp.bfloat16)

    arrive(full.at[c, pl.ds(0, OWNERS - 1)], 10)
    copy(full.at[c], full.at[c], 11, other).start()
    sends.append((full.at[0], 11))
    arrive(full.at[1 - c], 11)
    for ref, n in sends:
        copy(ref, ref, n, other).wait_send()


def finish(
    out_ref, ig_ref, full,
    out_hbm, ig_hbm, pg_hbm, rg_hbm, sg_hbm,
    pg_ref, rg_ref, sg_ref, sem,
):
    def write(src, dst, i):
        done = pltpu.make_async_copy(src, dst, sem.at[i])
        done.start()
        return done

    writes = [write(out_ref, out_hbm, 0), write(ig_ref, ig_hbm, 1)]
    squares = jnp.zeros((3, 4, 128), F32)
    for half_id in range(2):
        for o in range(OWNERS):
            v = full[half_id, o]
            squares = squares + v * v
    squares = squares[0] + squares[1] + squares[2]
    norm = jnp.sqrt(jnp.sum(jnp.sum(squares, axis=0, keepdims=True), axis=1, keepdims=True))
    factor = jnp.minimum(1.0, CEILING / (norm + 1e-06))
    for half_id in range(2):
        cols = slice(128 * half_id, 128 * half_id + 128)
        for o in range(OWNERS):
            for q in range(2):
                row = 8 * o + 4 * q
                pg_ref[row : row + 4, cols] = full[half_id, o, q] * factor
        for o in range(16):
            row = 4 * (o % 8)
            rg_ref[o // 8, row : row + 4, cols] = full[half_id, o, 2] * factor
        sg_ref[:, cols] = full[half_id, 16, 2, 0:1, :] * factor
    writes += [write(pg_ref, pg_hbm, 2), write(rg_ref, rg_hbm, 3), write(sg_ref, sg_hbm, 4)]
    for done in writes:
        done.wait()


def shards(inputs, cotangent, decay_rate, rotation, readout, skip_gain, projection):
    bf16 = jnp.bfloat16
    row, state, square = (RUN, CHANNELS), (2, STATES, CHANNELS), (CHANNELS, CHANNELS)
    pieces = (GROUP, 16, 128)
    sums = (2, OWNERS, 3, 4, 128)
    vmem = pl.BlockSpec(memory_space=pltpu.VMEM)
    hbm = pl.BlockSpec(memory_space=pltpu.HBM)
    operands = [
        pltpu.VMEM(row, bf16), pltpu.VMEM(row, bf16), pltpu.VMEM(state[1:], F32),
        pltpu.VMEM(state[1:], F32), pltpu.VMEM(state, F32), pltpu.VMEM((1, CHANNELS), F32),
        pltpu.VMEM(square, bf16),
    ]
    shapes = [row] * 5 + [(16,) + state, state, state, pieces, pieces]
    shapes += [(2 * GROUP, 16, 128), (2,) + pieces, (2, 16, 128)] + [pieces] * 6
    shapes += [(2, OWNERS, 2, 4, 128), (2, 17, 4, 128), (OWNERS, 2, 4, 128), (17, 4, 128)]
    shapes += [sums[1:], sums[1:], (1, 3, 4, 128), (BLOCKS, 3, 4, 128)]
    out, in_grad, total = pl.pallas_call(
        kernel,
        out_shape=(
            jax.ShapeDtypeStruct(row, bf16),
            jax.ShapeDtypeStruct(row, bf16),
            jax.ShapeDtypeStruct(sums, F32),
        ),
        in_specs=[hbm] * 7,
        out_specs=[vmem] * 3,
        scratch_shapes=operands
        + [pltpu.VMEM(shape, F32) for shape in shapes]
        + [pltpu.SemaphoreType.DMA((7,)), pltpu.SemaphoreType.DMA((13,)), pltpu.SemaphoreType.DMA((13,)), pltpu.SemaphoreType.REGULAR],
        compiler_params=pltpu.CompilerParams(
            collective_id=0, has_side_effects=True, vmem_limit_bytes=32 << 20
        ),
        name="layer",
    )(
        *(
            pltpu.with_memory_space_constraint(v, pltpu.HBM)
            for v in (
                inputs[0], cotangent[0], decay_rate, rotation, readout,
                skip_gain.reshape(1, CHANNELS), projection,
            )
        )
    )
    outs = pl.pallas_call(
        finish,
        out_shape=(
            jax.ShapeDtypeStruct(row, bf16),
            jax.ShapeDtypeStruct(row, bf16),
            jax.ShapeDtypeStruct(square, F32),
            jax.ShapeDtypeStruct(state, F32),
            jax.ShapeDtypeStruct((1, CHANNELS), F32),
        ),
        in_specs=[vmem] * 3,
        out_specs=[hbm] * 5,
        scratch_shapes=[
            pltpu.VMEM(square, F32), pltpu.VMEM(state, F32), pltpu.VMEM((1, CHANNELS), F32),
            pltpu.SemaphoreType.DMA((5,)),
        ],
        compiler_params=pltpu.CompilerParams(vmem_limit_bytes=4 << 20),
        name="finish",
    )(out, in_grad, total)
    return outs[0][None], outs[1][None], outs[2], outs[3], outs[4].reshape(CHANNELS)


def solution(mesh):
    split = P("batch", "seq", None)
    return jax.shard_map(
        shards,
        mesh=mesh,
        in_specs=(split, split, P(), P(), P(), P(), P()),
        out_specs=(split, split, P(), P(), P()),
        check_vma=False,
    )
```

```python
import math

import jax
import jax.numpy as jnp
import numpy as np
from jax import lax
from jax.experimental import pallas as pl
from jax.experimental.pallas import tpu as pltpu
from jax.sharding import PartitionSpec as P

MESH = pl.DeviceIdType.MESH
F32 = jnp.float32
STATES, CHANNELS, RUN = 32, 256, 128
GROUP = 8
BLOCKS = 8
OWNERS = 32

TURN_HI = 6.28125
TURN_MID = round((2 * math.pi - TURN_HI) * 2**20) / 2**20
TURN_LO = 2 * math.pi - TURN_HI - TURN_MID
GELU_SCALE = math.sqrt(2 / math.pi)
GELU_CUBE = 0.044715
CEILING = math.sqrt(CHANNELS * CHANNELS + 2 * STATES * CHANNELS + CHANNELS)


def hops(k):
    return k // 16 + min(k // 4 % 4, 4 - k // 4 % 4) + min(k % 4, 4 - k % 4)


FAR_FIRST = sorted(range(1, OWNERS), key=lambda k: (-hops(k), k))


def cmul(a, b):
    return a[0] * b[0] - a[1] * b[1], a[0] * b[1] + a[1] * b[0]


def decay_power(decay, rotation, times):
    angle = rotation * float(times)
    if times > 1:
        turns = jnp.floor(angle * (0.5 / math.pi) + 0.5)
        angle = ((angle - turns * TURN_HI) - turns * TURN_MID) - turns * TURN_LO
    size = jnp.exp(decay * -float(times))
    return size * jnp.cos(angle), size * jnp.sin(angle)


def entry_gain(decay):
    y = 2.0 * decay
    series = 1.0 - y * (1.0 / 8)
    for k in (7, 6, 5, 4, 3, 2):
        series = 1.0 - y * (1.0 / k) * series
    return jnp.sqrt(jnp.where(y < 0.25, y * series, 1.0 - jnp.exp(-y)))


def put_pieces(ref, value):
    re, im = value
    for p in range(GROUP):
        rows, cols = slice(8 * (p // 2), 8 * (p // 2) + 8), slice(128 * (p % 2), 128 * (p % 2) + 128)
        ref[p, 0:8, :] = re[rows, cols]
        ref[p, 8:16, :] = im[rows, cols]


def get_pieces(ref):
    def part(lo):
        return jnp.concatenate(
            [
                jnp.concatenate([ref[2 * n, lo : lo + 8, :], ref[2 * n + 1, lo : lo + 8, :]], axis=1)
                for n in range(4)
            ],
            axis=0,
        )

    return part(0), part(8)


def load(ref, i):
    return ref[i, 0:8, :], ref[i, 8:16, :]


def store(ref, i, value):
    ref[i, 0:8, :] = value[0]
    ref[i, 8:16, :] = value[1]


def kernel(
    x_hbm, cot_hbm, decay_hbm, rot_hbm, read_hbm, skip_hbm, proj_hbm,
    out_ref, ig_ref, full,
    x_ref, cot_ref, decay_ref, rot_ref, read_ref, skip_ref, proj_ref,
    xf, gf, mix, hb, il,
    tab, lam_s, cof_s, l128, l1024,
    e_buf, o_buf, t_buf, r1f, r2f, hin, r1b, r2b, lin,
    pb, gb, ra1p, ra1g, a2s, ra2, pc, ra3,
    isem, ssem, rsem, far_sem,
):
    s, b = lax.axis_index("seq"), lax.axis_index("batch")
    g, blk = lax.rem(s, GROUP), lax.div(s, GROUP)
    y, c = lax.div(b, 2), lax.rem(b, 2)
    me = lax.div(g, 4) * 16 + lax.rem(g, 4) * 4 + y

    base = blk * GROUP
    zs = [lax.rem(lax.div(g, 4) + k, 2) for k in range(2)]
    xs = [lax.rem(lax.rem(g, 4) + k, 4) for k in range(4)]
    ys = [lax.rem(y + k, 4) for k in range(4)]
    seqs = [[base + z * 4 + x for x in xs] for z in zs]
    batches = [v * 2 + c for v in ys]
    in_block = [
        (zs[k // 4] * 4 + xs[k % 4], {"seq": seqs[k // 4][k % 4], "batch": b})
        for k in (6, 5, 7, 2, 4, 1, 3)
    ]
    across = [{"seq": lax.rem(blk + k, BLOCKS) * GROUP + g, "batch": b} for k in range(BLOCKS)]
    owners = [
        (
            zs[k // 16] * 16 + xs[k // 4 % 4] * 4 + ys[k % 4],
            {"seq": seqs[k // 16][k // 4 % 4], "batch": batches[k % 4]},
        )
        for k in FAR_FIRST
    ]
    other = {"seq": s, "batch": y * 2 + (1 - c)}

    fetches = [
        pltpu.make_async_copy(src, dst, isem.at[i])
        for i, (src, dst) in enumerate(
            [(decay_hbm, decay_ref), (rot_hbm, rot_ref), (read_hbm, read_ref), (x_hbm, x_ref),
             (skip_hbm, skip_ref), (cot_hbm, cot_ref), (proj_hbm, proj_ref)]
        )
    ]
    for fetch in fetches:
        fetch.start()

    barrier = pltpu.get_barrier_semaphore()
    partners = [across[k] for k in (2, 6, 1, 7)] + [device for _, device in in_block]
    partners += [{"seq": s, "batch": batch} for batch in batches[1:]] + [other]

    def greet(sem, devices):
        for device in devices:
            pl.semaphore_signal(sem, inc=1, device_id=device, device_id_type=MESH)

    greet(barrier, partners)

    def copy(src, dst, n, device):
        return pltpu.make_async_remote_copy(
            src_ref=src, dst_ref=dst, send_sem=ssem.at[n], recv_sem=rsem.at[n],
            device_id=device, device_id_type=MESH,
        )

    for fetch in fetches:
        fetch.wait()

    decay, rot = decay_ref[...], rot_ref[...]
    gain = entry_gain(decay)
    lam = decay_power(decay, rot, 1)
    put_pieces(l128, decay_power(decay, rot, RUN))
    put_pieces(l1024, decay_power(decay, rot, RUN * GROUP))
    lam_s[0], lam_s[1] = lam
    cof_s[0] = gain * read_ref[0]
    cof_s[1] = gain * read_ref[1]
    xf[...] = x_ref[...].astype(F32)
    row_id = lax.broadcasted_iota(jnp.int32, (8, CHANNELS), 0)
    zero = jnp.zeros((STATES, CHANNELS), F32)

    def sweep(carry, body, backward=False, lo=0, hi=RUN // 8):
        def step(i, carry):
            first = RUN - 8 - 8 * i if backward else 8 * i
            return body(pl.multiple_of(first, 8), carry)

        return lax.fori_loop(lo, hi, step, carry)

    order = tuple(range(8))

    def fwd_state(first, carry):
        lam_re, lam_im = lam_s[0], lam_s[1]
        rows = xf[pl.ds(first, 8), :]
        re, im = carry
        for j in order:
            re, im = lam_re * re - lam_im * im + rows[j : j + 1, :], lam_re * im + lam_im * re
        return re, im

    def fwd_local(first, carry):
        lam_re, lam_im = lam_s[0], lam_s[1]
        cof_re, cof_im = cof_s[0], cof_s[1]
        rows = xf[pl.ds(first, 8), :]
        re, im = carry
        acc = jnp.zeros((8, CHANNELS), F32)
        for j in order:
            re, im = lam_re * re - lam_im * im + rows[j : j + 1, :], lam_re * im + lam_im * re
            total = jnp.sum(cof_re * re - cof_im * im, axis=0, keepdims=True)
            acc = jnp.where(row_id == j, total, acc)
        mix[pl.ds(first, 8), :] = acc + rows * skip_ref[...]
        return re, im

    re, im = sweep((zero, zero), fwd_state)
    put_pieces(e_buf, (gain * re, gain * im))
    pl.semaphore_wait(barrier, len(partners))

    sends = []

    def scatter(buf, dst, n):
        dst[g] = buf[g]
        for p, device in in_block:
            copy(buf.at[p], dst.at[g], n, device).start()
        sends.append((buf.at[pl.ds(0, GROUP - 1)], n))

    def spread(src, dst, n):
        dst[blk] = src[...]
        for k in (4, 5, 3, 6, 2, 7, 1):
            copy(src, dst.at[blk], n, across[k]).start()
        sends.append((dst.at[pl.ds(0, BLOCKS - 1)], n))

    def arrive(ref, n):
        copy(ref, ref, n, other).wait_recv()

    def block_total(r1, turn):
        step = load(l128, g)
        total = load(r1, turn[0])
        for i in turn[1:]:
            moved = cmul(step, total)
            nxt = load(r1, i)
            total = moved[0] + nxt[0], moved[1] + nxt[1]
        return total

    def entering(r1, r2, buf, turn, backward):
        step, leap = load(l128, g), load(l1024, g)
        state = (jnp.zeros((8, 128), F32), jnp.zeros((8, 128), F32))
        for i in turn:
            moved, nxt = cmul(leap, state), load(r2, i)
            use = (i > blk) if backward else (i < blk)
            state = tuple(jnp.where(use, m + v, old) for m, v, old in zip(moved, nxt, state))
        for i in turn:
            store(buf, i, state)
            moved, nxt = cmul(step, state), load(r1, i)
            state = moved[0] + nxt[0], moved[1] + nxt[1]

    up, down = tuple(range(8)), tuple(range(7, -1, -1))
    seven = pl.ds(0, 7)

    greet(far_sem, (across[2], across[6]))
    scatter(e_buf, r1f, 0)
    sweep((zero, zero), fwd_local)
    hb[...] = lax.dot_general(
        cot_ref[...], proj_ref[...], (((1,), (1,)), ((), ())), preferred_element_type=F32
    )
    pl.semaphore_wait(far_sem, 2)
    arrive(r1f.at[seven], 0)
    t = block_total(r1f, up)
    t_buf[0, 0:8, :], t_buf[0, 8:16, :] = t
    spread(t_buf.at[0], r2f, 1)

    def fill_table(j, power):
        tab[j, 0], tab[j, 1] = power
        return cmul((lam_s[0], lam_s[1]), power)

    lax.fori_loop(0, 16, fill_table, (lam_s[0], lam_s[1]))
    gb[...] = jnp.zeros_like(gb)
    a2s[...] = jnp.zeros_like(a2s)
    arrive(r2f.at[seven], 1)
    entering(r1f, r2f, o_buf.at[0], up, False)
    scatter(o_buf.at[0], hin, 2)
    arrive(hin.at[seven], 2)

    enter = get_pieces(hin)
    carried = cmul((read_ref[0], read_ref[1]), enter)

    def inject(carried, ref, backward):
        def step(i, carry):
            re, im = carry
            for part in range(2):
                first = 16 * i + 8 * part
                acc = jnp.zeros((8, CHANNELS), F32)
                for j in order:
                    n = 8 * part + j
                    total = jnp.sum(tab[n, 0] * re - tab[n, 1] * im, axis=0, keepdims=True)
                    acc = jnp.where(row_id == (7 - j if backward else j), total, acc)
                first = pl.multiple_of(RUN - 8 - first if backward else first, 8)
                ref[pl.ds(first, 8), :] = ref[pl.ds(first, 8), :] + acc
            return cmul((tab[15, 0], tab[15, 1]), carry)

        lax.fori_loop(0, RUN // 16, step, carried)

    inject(carried, mix, False)

    mixed = mix[...]
    square = mixed * mixed
    tanh = jnp.tanh(GELU_SCALE * (mixed + GELU_CUBE * (mixed * square)))
    half = 0.5 * (1.0 + tanh)
    hidden = (mixed * half).astype(jnp.bfloat16)
    slope = half + (0.5 * mixed) * (1.0 - tanh * tanh) * (
        GELU_SCALE * (1.0 + (3.0 * GELU_CUBE) * square)
    )
    grad = hb[...] * slope
    gf[...] = grad
    part = lax.dot_general(
        hidden, cot_ref[...], (((0,), (0,)), ((), ())), preferred_element_type=F32
    )
    for half_id in range(2):
        for o in range(OWNERS):
            for q in range(2):
                row = 8 * o + 4 * q
                pb[half_id, o, q] = part[row : row + 4, 128 * half_id : 128 * half_id + 128]
    copy(pb.at[1 - c], ra1p, 3, other).start()
    sends.append((pb.at[0], 3))

    def bwd_local(first, carry):
        lam_re, lam_im = lam_s[0], lam_s[1]
        rows, xs = gf[pl.ds(first, 8), :], xf[pl.ds(first, 8), :]
        re, im, sum_re, sum_im = carry
        for j in reversed(order):
            re, im = lam_re * re - lam_im * im + rows[j : j + 1, :], lam_re * im + lam_im * re
            sum_re = sum_re + xs[j : j + 1, :] * re
            sum_im = sum_im + xs[j : j + 1, :] * im
        return re, im, sum_re, sum_im

    re, im, sum_re, sum_im = sweep((zero, zero, zero, zero), bwd_local, True)
    lam = lam_s[0], lam_s[1]
    extra = cmul(cmul(lam, (re, im)), get_pieces(hin))
    read_re = gain * sum_re + extra[0]
    read_im = -(gain * sum_im + extra[1])
    skip_part = jnp.sum(gf[...] * xf[...], axis=0, keepdims=True)
    for half_id in range(2):
        cols = slice(128 * half_id, 128 * half_id + 128)
        for o in range(16):
            gb[half_id, o] = (read_re if o < 8 else read_im)[4 * (o % 8) : 4 * (o % 8) + 4, cols]
        gb[half_id, 16, 0:1, :] = skip_part[:, cols]
    copy(gb.at[1 - c], ra1g, 5, other).start()
    sends.append((gb.at[0], 5))
    put_pieces(e_buf.at[pl.ds(GROUP, GROUP)], (re, im))
    scatter(e_buf.at[pl.ds(GROUP, GROUP)], r1b, 4)
    arrive(ra1p, 3)
    for o in range(OWNERS):
        a2s[o, 0:2] = pb[c, o] + ra1p[o]
    ra2[me, 0:2] = a2s[me, 0:2]
    for o, device in owners:
        copy(a2s.at[o, pl.ds(0, 2)], ra2.at[me, pl.ds(0, 2)], 6, device).start()
    sends.append((ra1p.at[pl.ds(0, OWNERS - 1)], 6))
    arrive(ra1g, 5)
    for o in range(17):
        a2s[o, 2] = gb[c, o] + ra1g[o]
    ra2[me, 2] = a2s[me, 2]
    for o, device in owners:
        copy(a2s.at[o, 2], ra2.at[me, 2], 12, device).start()
    sends.append((ra2.at[pl.ds(0, OWNERS - 1), 2], 12))

    arrive(r1b.at[seven], 4)
    t = block_total(r1b, down)
    t_buf[1, 0:8, :], t_buf[1, 8:16, :] = t
    spread(t_buf.at[1], r2b, 7)


    arrive(ra2.at[pl.ds(0, OWNERS - 1), pl.ds(0, 2)], 6)
    arrive(ra2.at[pl.ds(0, OWNERS - 1), 2], 12)
    terms = [ra2[o] for o in range(OWNERS)]
    while len(terms) > 1:
        terms = [a + b for a, b in zip(terms[::2], terms[1::2])]
    pc[0] = terms[0]
    spread(pc.at[0], ra3, 8)

    out_ref[...] = (
        xf[...] + jnp.dot(hidden, proj_ref[...], preferred_element_type=F32)
    ).astype(jnp.bfloat16)

    def bwd_read(first, carry):
        lam_re, lam_im = lam_s[0], lam_s[1]
        cof_re, cof_im = cof_s[0], cof_s[1]
        rows = gf[pl.ds(first, 8), :]
        re, im = carry
        acc = jnp.zeros((8, CHANNELS), F32)
        for j in reversed(order):
            re, im = lam_re * re - lam_im * im + rows[j : j + 1, :], lam_re * im + lam_im * re
            total = jnp.sum(cof_re * re - cof_im * im, axis=0, keepdims=True)
            acc = jnp.where(row_id == j, total, acc)
        il[pl.ds(first, 8), :] = acc + rows * skip_ref[...]
        return re, im

    sweep((zero, zero), bwd_read, True)
    il[...] = il[...] + cot_ref[...].astype(F32)

    arrive(r2b.at[seven], 7)
    entering(r1b, r2b, o_buf.at[1], down, True)
    scatter(o_buf.at[1], lin, 9)

    arrive(ra3.at[seven], 8)
    total = ra3[0]
    for o in range(1, BLOCKS):
        total = total + ra3[o]
    full[c, me] = total
    for _, device in owners:
        copy(full.at[c, me], full.at[c, me], 10, device).start()
    sends.append((ra2.at[pl.ds(0, OWNERS - 1)], 10))

    arrive(lin.at[seven], 9)
    carried = cmul((cof_s[0], cof_s[1]), get_pieces(lin))

    inject(carried, il, True)
    ig_ref[...] = il[...].astype(jnp.bfloat16)

    arrive(full.at[c, pl.ds(0, OWNERS - 1)], 10)
    copy(full.at[c], full.at[c], 11, other).start()
    sends.append((full.at[0], 11))
    arrive(full.at[1 - c], 11)
    for ref, n in sends:
        copy(ref, ref, n, other).wait_send()


def finish(
    out_ref, ig_ref, full,
    out_hbm, ig_hbm, pg_hbm, rg_hbm, sg_hbm,
    pg_ref, rg_ref, sg_ref, sem,
):
    def write(src, dst, i):
        done = pltpu.make_async_copy(src, dst, sem.at[i])
        done.start()
        return done

    writes = [write(out_ref, out_hbm, 0), write(ig_ref, ig_hbm, 1)]
    squares = jnp.zeros((3, 4, 128), F32)
    for half_id in range(2):
        for o in range(OWNERS):
            v = full[half_id, o]
            squares = squares + v * v
    squares = squares[0] + squares[1] + squares[2]
    norm = jnp.sqrt(jnp.sum(jnp.sum(squares, axis=0, keepdims=True), axis=1, keepdims=True))
    factor = jnp.minimum(1.0, CEILING / (norm + 1e-06))
    for half_id in range(2):
        cols = slice(128 * half_id, 128 * half_id + 128)
        for o in range(OWNERS):
            for q in range(2):
                row = 8 * o + 4 * q
                pg_ref[row : row + 4, cols] = full[half_id, o, q] * factor
        for o in range(16):
            row = 4 * (o % 8)
            rg_ref[o // 8, row : row + 4, cols] = full[half_id, o, 2] * factor
        sg_ref[:, cols] = full[half_id, 16, 2, 0:1, :] * factor
    writes += [write(pg_ref, pg_hbm, 2), write(rg_ref, rg_hbm, 3), write(sg_ref, sg_hbm, 4)]
    for done in writes:
        done.wait()


def shards(inputs, cotangent, decay_rate, rotation, readout, skip_gain, projection):
    bf16 = jnp.bfloat16
    row, state, square = (RUN, CHANNELS), (2, STATES, CHANNELS), (CHANNELS, CHANNELS)
    pieces = (GROUP, 16, 128)
    sums = (2, OWNERS, 3, 4, 128)
    vmem = pl.BlockSpec(memory_space=pltpu.VMEM)
    hbm = pl.BlockSpec(memory_space=pltpu.HBM)
    operands = [
        pltpu.VMEM(row, bf16), pltpu.VMEM(row, bf16), pltpu.VMEM(state[1:], F32),
        pltpu.VMEM(state[1:], F32), pltpu.VMEM(state, F32), pltpu.VMEM((1, CHANNELS), F32),
        pltpu.VMEM(square, bf16),
    ]
    shapes = [row] * 5 + [(16,) + state, state, state, pieces, pieces]
    shapes += [(2 * GROUP, 16, 128), (2,) + pieces, (2, 16, 128)] + [pieces] * 6
    shapes += [(2, OWNERS, 2, 4, 128), (2, 17, 4, 128), (OWNERS, 2, 4, 128), (17, 4, 128)]
    shapes += [sums[1:], sums[1:], (1, 3, 4, 128), (BLOCKS, 3, 4, 128)]
    out, in_grad, total = pl.pallas_call(
        kernel,
        out_shape=(
            jax.ShapeDtypeStruct(row, bf16),
            jax.ShapeDtypeStruct(row, bf16),
            jax.ShapeDtypeStruct(sums, F32),
        ),
        in_specs=[hbm] * 7,
        out_specs=[vmem] * 3,
        scratch_shapes=operands
        + [pltpu.VMEM(shape, F32) for shape in shapes]
        + [pltpu.SemaphoreType.DMA((7,)), pltpu.SemaphoreType.DMA((13,)), pltpu.SemaphoreType.DMA((13,)), pltpu.SemaphoreType.REGULAR],
        compiler_params=pltpu.CompilerParams(
            collective_id=0, has_side_effects=True, vmem_limit_bytes=32 << 20
        ),
        name="layer",
    )(
        *(
            pltpu.with_memory_space_constraint(v, pltpu.HBM)
            for v in (
                inputs[0], cotangent[0], decay_rate, rotation, readout,
                skip_gain.reshape(1, CHANNELS), projection,
            )
        )
    )
    outs = pl.pallas_call(
        finish,
        out_shape=(
            jax.ShapeDtypeStruct(row, bf16),
            jax.ShapeDtypeStruct(row, bf16),
            jax.ShapeDtypeStruct(square, F32),
            jax.ShapeDtypeStruct(state, F32),
            jax.ShapeDtypeStruct((1, CHANNELS), F32),
        ),
        in_specs=[vmem] * 3,
        out_specs=[hbm] * 5,
        scratch_shapes=[
            pltpu.VMEM(square, F32), pltpu.VMEM(state, F32), pltpu.VMEM((1, CHANNELS), F32),
            pltpu.SemaphoreType.DMA((5,)),
        ],
        compiler_params=pltpu.CompilerParams(vmem_limit_bytes=4 << 20),
        name="finish",
    )(out, in_grad, total)
    return outs[0][None], outs[1][None], outs[2], outs[3], outs[4].reshape(CHANNELS)


def solution(mesh):
    split = P("batch", "seq", None)
    return jax.shard_map(
        shards,
        mesh=mesh,
        in_specs=(split, split, P(), P(), P(), P(), P()),
        out_specs=(split, split, P(), P(), P()),
        check_vma=False,
    )
```

```python
import math

import jax
import jax.numpy as jnp
import numpy as np
from jax import lax
from jax.experimental import pallas as pl
from jax.experimental.pallas import tpu as pltpu
from jax.sharding import PartitionSpec as P

MESH = pl.DeviceIdType.MESH
F32 = jnp.float32
STATES, CHANNELS, RUN = 32, 256, 128
GROUP = 8
BLOCKS = 8
OWNERS = 32

TURN_HI = 6.28125
TURN_MID = round((2 * math.pi - TURN_HI) * 2**20) / 2**20
TURN_LO = 2 * math.pi - TURN_HI - TURN_MID
GELU_SCALE = math.sqrt(2 / math.pi)
GELU_CUBE = 0.044715
CEILING = math.sqrt(CHANNELS * CHANNELS + 2 * STATES * CHANNELS + CHANNELS)


def hops(k):
    return k // 16 + min(k // 4 % 4, 4 - k // 4 % 4) + min(k % 4, 4 - k % 4)


FAR_FIRST = sorted(range(1, OWNERS), key=lambda k: (-hops(k), k))


def cmul(a, b):
    return a[0] * b[0] - a[1] * b[1], a[0] * b[1] + a[1] * b[0]


def decay_power(decay, rotation, times):
    angle = rotation * float(times)
    if times > 1:
        turns = jnp.floor(angle * (0.5 / math.pi) + 0.5)
        angle = ((angle - turns * TURN_HI) - turns * TURN_MID) - turns * TURN_LO
    size = jnp.exp(decay * -float(times))
    return size * jnp.cos(angle), size * jnp.sin(angle)


def entry_gain(decay):
    y = 2.0 * decay
    series = 1.0 - y * (1.0 / 8)
    for k in (7, 6, 5, 4, 3, 2):
        series = 1.0 - y * (1.0 / k) * series
    return jnp.sqrt(jnp.where(y < 0.25, y * series, 1.0 - jnp.exp(-y)))


def put_pieces(ref, value):
    re, im = value
    for p in range(GROUP):
        rows, cols = slice(8 * (p // 2), 8 * (p // 2) + 8), slice(128 * (p % 2), 128 * (p % 2) + 128)
        ref[p, 0:8, :] = re[rows, cols]
        ref[p, 8:16, :] = im[rows, cols]


def get_pieces(ref):
    def part(lo):
        return jnp.concatenate(
            [
                jnp.concatenate([ref[2 * n, lo : lo + 8, :], ref[2 * n + 1, lo : lo + 8, :]], axis=1)
                for n in range(4)
            ],
            axis=0,
        )

    return part(0), part(8)


def load(ref, i):
    return ref[i, 0:8, :], ref[i, 8:16, :]


def store(ref, i, value):
    ref[i, 0:8, :] = value[0]
    ref[i, 8:16, :] = value[1]


def kernel(
    x_hbm, cot_hbm, decay_hbm, rot_hbm, read_hbm, skip_hbm, proj_hbm,
    out_ref, ig_ref, full,
    x_ref, cot_ref, decay_ref, rot_ref, read_ref, skip_ref, proj_ref,
    xf, gf, mix, hb, il,
    tab, lam_s, cof_s, l128, l1024,
    e_buf, o_buf, t_buf, r1f, r2f, hin, r1b, r2b, lin,
    pb, gb, ra1p, ra1g, a2s, ra2, pc, ra3,
    isem, ssem, rsem, far_sem,
):
    s, b = lax.axis_index("seq"), lax.axis_index("batch")
    g, blk = lax.rem(s, GROUP), lax.div(s, GROUP)
    y, c = lax.div(b, 2), lax.rem(b, 2)
    me = lax.div(g, 4) * 16 + lax.rem(g, 4) * 4 + y

    base = blk * GROUP
    zs = [lax.rem(lax.div(g, 4) + k, 2) for k in range(2)]
    xs = [lax.rem(lax.rem(g, 4) + k, 4) for k in range(4)]
    ys = [lax.rem(y + k, 4) for k in range(4)]
    seqs = [[base + z * 4 + x for x in xs] for z in zs]
    batches = [v * 2 + c for v in ys]
    in_block = [
        (zs[k // 4] * 4 + xs[k % 4], {"seq": seqs[k // 4][k % 4], "batch": b})
        for k in (6, 5, 7, 2, 4, 1, 3)
    ]
    across = [{"seq": lax.rem(blk + k, BLOCKS) * GROUP + g, "batch": b} for k in range(BLOCKS)]
    owners = [
        (
            zs[k // 16] * 16 + xs[k // 4 % 4] * 4 + ys[k % 4],
            {"seq": seqs[k // 16][k // 4 % 4], "batch": batches[k % 4]},
        )
        for k in FAR_FIRST
    ]
    other = {"seq": s, "batch": y * 2 + (1 - c)}

    fetches = [
        pltpu.make_async_copy(src, dst, isem.at[i])
        for i, (src, dst) in enumerate(
            [(decay_hbm, decay_ref), (rot_hbm, rot_ref), (read_hbm, read_ref), (x_hbm, x_ref),
             (skip_hbm, skip_ref), (cot_hbm, cot_ref), (proj_hbm, proj_ref)]
        )
    ]
    for fetch in fetches:
        fetch.start()

    barrier = pltpu.get_barrier_semaphore()
    partners = [across[k] for k in (2, 6, 1, 7)] + [device for _, device in in_block]
    partners += [{"seq": s, "batch": batch} for batch in batches[1:]] + [other]

    def greet(sem, devices):
        for device in devices:
            pl.semaphore_signal(sem, inc=1, device_id=device, device_id_type=MESH)

    greet(barrier, partners)

    def copy(src, dst, n, device):
        return pltpu.make_async_remote_copy(
            src_ref=src, dst_ref=dst, send_sem=ssem.at[n], recv_sem=rsem.at[n],
            device_id=device, device_id_type=MESH,
        )

    for fetch in fetches:
        fetch.wait()

    decay, rot = decay_ref[...], rot_ref[...]
    gain = entry_gain(decay)
    lam = decay_power(decay, rot, 1)
    put_pieces(l128, decay_power(decay, rot, RUN))
    put_pieces(l1024, decay_power(decay, rot, RUN * GROUP))
    lam_s[0], lam_s[1] = lam
    cof_s[0] = gain * read_ref[0]
    cof_s[1] = gain * read_ref[1]
    xf[...] = x_ref[...].astype(F32)
    row_id = lax.broadcasted_iota(jnp.int32, (8, CHANNELS), 0)
    zero = jnp.zeros((STATES, CHANNELS), F32)

    def sweep(carry, body, backward=False, lo=0, hi=RUN // 8):
        def step(i, carry):
            first = RUN - 8 - 8 * i if backward else 8 * i
            return body(pl.multiple_of(first, 8), carry)

        return lax.fori_loop(lo, hi, step, carry)

    order = tuple(range(8))

    def fwd_state(first, carry):
        lam_re, lam_im = lam_s[0], lam_s[1]
        rows = xf[pl.ds(first, 8), :]
        re, im = carry
        for j in order:
            re, im = lam_re * re - lam_im * im + rows[j : j + 1, :], lam_re * im + lam_im * re
        return re, im

    def fwd_local(first, carry):
        lam_re, lam_im = lam_s[0], lam_s[1]
        cof_re, cof_im = cof_s[0], cof_s[1]
        rows = xf[pl.ds(first, 8), :]
        re, im = carry
        acc = jnp.zeros((8, CHANNELS), F32)
        for j in order:
            re, im = lam_re * re - lam_im * im + rows[j : j + 1, :], lam_re * im + lam_im * re
            total = jnp.sum(cof_re * re - cof_im * im, axis=0, keepdims=True)
            acc = jnp.where(row_id == j, total, acc)
        mix[pl.ds(first, 8), :] = acc + rows * skip_ref[...]
        return re, im

    re, im = sweep((zero, zero), fwd_state)
    put_pieces(e_buf, (gain * re, gain * im))
    pl.semaphore_wait(barrier, len(partners))

    sends = []

    def scatter(buf, dst, n):
        dst[g] = buf[g]
        for p, device in in_block:
            copy(buf.at[p], dst.at[g], n, device).start()
        sends.append((buf.at[pl.ds(0, GROUP - 1)], n))

    def spread(src, dst, n):
        dst[blk] = src[...]
        for k in (4, 5, 3, 6, 2, 7, 1):
            copy(src, dst.at[blk], n, across[k]).start()
        sends.append((dst.at[pl.ds(0, BLOCKS - 1)], n))

    def arrive(ref, n):
        copy(ref, ref, n, other).wait_recv()

    def block_total(r1, turn):
        step = load(l128, g)
        total = load(r1, turn[0])
        for i in turn[1:]:
            moved = cmul(step, total)
            nxt = load(r1, i)
            total = moved[0] + nxt[0], moved[1] + nxt[1]
        return total

    def entering(r1, r2, buf, turn, backward):
        step, leap = load(l128, g), load(l1024, g)
        state = (jnp.zeros((8, 128), F32), jnp.zeros((8, 128), F32))
        for i in turn:
            moved, nxt = cmul(leap, state), load(r2, i)
            use = (i > blk) if backward else (i < blk)
            state = tuple(jnp.where(use, m + v, old) for m, v, old in zip(moved, nxt, state))
        for i in turn:
            store(buf, i, state)
            moved, nxt = cmul(step, state), load(r1, i)
            state = moved[0] + nxt[0], moved[1] + nxt[1]

    up, down = tuple(range(8)), tuple(range(7, -1, -1))
    seven = pl.ds(0, 7)

    greet(far_sem, (across[2], across[6]))
    scatter(e_buf, r1f, 0)
    sweep((zero, zero), fwd_local)
    hb[...] = lax.dot_general(
        cot_ref[...], proj_ref[...], (((1,), (1,)), ((), ())), preferred_element_type=F32
    )
    pl.semaphore_wait(far_sem, 2)
    arrive(r1f.at[seven], 0)
    t = block_total(r1f, up)
    t_buf[0, 0:8, :], t_buf[0, 8:16, :] = t
    spread(t_buf.at[0], r2f, 1)

    def fill_table(j, power):
        tab[j, 0], tab[j, 1] = power
        return cmul((lam_s[0], lam_s[1]), power)

    lax.fori_loop(0, 16, fill_table, (lam_s[0], lam_s[1]))
    gb[...] = jnp.zeros_like(gb)
    a2s[...] = jnp.zeros_like(a2s)
    arrive(r2f.at[seven], 1)
    entering(r1f, r2f, o_buf.at[0], up, False)
    scatter(o_buf.at[0], hin, 2)
    arrive(hin.at[seven], 2)

    enter = get_pieces(hin)
    carried = cmul((read_ref[0], read_ref[1]), enter)

    def inject(carried, ref, backward):
        def step(i, carry):
            re, im = carry
            for part in range(2):
                first = 16 * i + 8 * part
                acc = jnp.zeros((8, CHANNELS), F32)
                for j in order:
                    n = 8 * part + j
                    total = jnp.sum(tab[n, 0] * re - tab[n, 1] * im, axis=0, keepdims=True)
                    acc = jnp.where(row_id == (7 - j if backward else j), total, acc)
                first = pl.multiple_of(RUN - 8 - first if backward else first, 8)
                ref[pl.ds(first, 8), :] = ref[pl.ds(first, 8), :] + acc
            return cmul((tab[15, 0], tab[15, 1]), carry)

        lax.fori_loop(0, RUN // 16, step, carried)

    inject(carried, mix, False)

    mixed = mix[...]
    square = mixed * mixed
    tanh = jnp.tanh(GELU_SCALE * (mixed + GELU_CUBE * (mixed * square)))
    half = 0.5 * (1.0 + tanh)
    hidden = (mixed * half).astype(jnp.bfloat16)
    slope = half + (0.5 * mixed) * (1.0 - tanh * tanh) * (
        GELU_SCALE * (1.0 + (3.0 * GELU_CUBE) * square)
    )
    grad = hb[...] * slope
    gf[...] = grad
    part = lax.dot_general(
        hidden, cot_ref[...], (((0,), (0,)), ((), ())), preferred_element_type=F32
    )
    for half_id in range(2):
        for o in range(OWNERS):
            for q in range(2):
                row = 8 * o + 4 * q
                pb[half_id, o, q] = part[row : row + 4, 128 * half_id : 128 * half_id + 128]
    copy(pb.at[1 - c], ra1p, 3, other).start()
    sends.append((pb.at[0], 3))

    def bwd_local(first, carry):
        lam_re, lam_im = lam_s[0], lam_s[1]
        rows, xs = gf[pl.ds(first, 8), :], xf[pl.ds(first, 8), :]
        re, im, sum_re, sum_im = carry
        for j in reversed(order):
            re, im = lam_re * re - lam_im * im + rows[j : j + 1, :], lam_re * im + lam_im * re
            sum_re = sum_re + xs[j : j + 1, :] * re
            sum_im = sum_im + xs[j : j + 1, :] * im
        return re, im, sum_re, sum_im

    re, im, sum_re, sum_im = sweep((zero, zero, zero, zero), bwd_local, True)
    lam = lam_s[0], lam_s[1]
    extra = cmul(cmul(lam, (re, im)), get_pieces(hin))
    read_re = gain * sum_re + extra[0]
    read_im = -(gain * sum_im + extra[1])
    skip_part = jnp.sum(gf[...] * xf[...], axis=0, keepdims=True)
    for half_id in range(2):
        cols = slice(128 * half_id, 128 * half_id + 128)
        for o in range(16):
            gb[half_id, o] = (read_re if o < 8 else read_im)[4 * (o % 8) : 4 * (o % 8) + 4, cols]
        gb[half_id, 16, 0:1, :] = skip_part[:, cols]
    copy(gb.at[1 - c], ra1g, 5, other).start()
    sends.append((gb.at[0], 5))
    put_pieces(e_buf.at[pl.ds(GROUP, GROUP)], (re, im))
    scatter(e_buf.at[pl.ds(GROUP, GROUP)], r1b, 4)
    arrive(ra1p, 3)
    for o in range(OWNERS):
        a2s[o, 0:2] = pb[c, o] + ra1p[o]
    arrive(ra1g, 5)
    for o in range(17):
        a2s[o, 2] = gb[c, o] + ra1g[o]
    ra2[me] = a2s[me]
    for o, device in owners:
        copy(a2s.at[o], ra2.at[me], 6, device).start()
    sends.append((ra2.at[pl.ds(0, OWNERS - 1)], 6))

    arrive(r1b.at[seven], 4)
    t = block_total(r1b, down)
    t_buf[1, 0:8, :], t_buf[1, 8:16, :] = t
    spread(t_buf.at[1], r2b, 7)


    arrive(ra2.at[pl.ds(0, OWNERS - 1)], 6)
    terms = [ra2[o] for o in range(OWNERS)]
    while len(terms) > 1:
        terms = [a + b for a, b in zip(terms[::2], terms[1::2])]
    pc[0] = terms[0]
    spread(pc.at[0], ra3, 8)

    out_ref[...] = (
        xf[...] + jnp.dot(hidden, proj_ref[...], preferred_element_type=F32)
    ).astype(jnp.bfloat16)

    def bwd_read(first, carry):
        lam_re, lam_im = lam_s[0], lam_s[1]
        cof_re, cof_im = cof_s[0], cof_s[1]
        rows = gf[pl.ds(first, 8), :]
        re, im = carry
        acc = jnp.zeros((8, CHANNELS), F32)
        for j in reversed(order):
            re, im = lam_re * re - lam_im * im + rows[j : j + 1, :], lam_re * im + lam_im * re
            total = jnp.sum(cof_re * re - cof_im * im, axis=0, keepdims=True)
            acc = jnp.where(row_id == j, total, acc)
        il[pl.ds(first, 8), :] = acc + rows * skip_ref[...]
        return re, im

    sweep((zero, zero), bwd_read, True)
    il[...] = il[...] + cot_ref[...].astype(F32)

    arrive(r2b.at[seven], 7)
    entering(r1b, r2b, o_buf.at[1], down, True)
    scatter(o_buf.at[1], lin, 9)

    arrive(ra3.at[seven], 8)
    total = ra3[0]
    for o in range(1, BLOCKS):
        total = total + ra3[o]
    full[c, me] = total
    for _, device in owners:
        far = {"seq": device["seq"], "batch": device["batch"] + (1 - 2 * c)}
        copy(full.at[c, me], full.at[c, me], 11, far).start()
        copy(full.at[c, me], full.at[c, me], 10, device).start()
    copy(full.at[c, me], full.at[c, me], 11, other).start()
    sends.append((ra2.at[pl.ds(0, OWNERS - 1)], 10))

    arrive(lin.at[seven], 9)
    carried = cmul((cof_s[0], cof_s[1]), get_pieces(lin))

    inject(carried, il, True)
    ig_ref[...] = il[...].astype(jnp.bfloat16)

    arrive(full.at[c, pl.ds(0, OWNERS - 1)], 10)
    sends.append((full.at[0], 11))
    arrive(full.at[1 - c], 11)
    for ref, n in sends:
        copy(ref, ref, n, other).wait_send()


def finish(
    out_ref, ig_ref, full,
    out_hbm, ig_hbm, pg_hbm, rg_hbm, sg_hbm,
    pg_ref, rg_ref, sg_ref, sem,
):
    def write(src, dst, i):
        done = pltpu.make_async_copy(src, dst, sem.at[i])
        done.start()
        return done

    writes = [write(out_ref, out_hbm, 0), write(ig_ref, ig_hbm, 1)]
    squares = jnp.zeros((3, 4, 128), F32)
    for half_id in range(2):
        for o in range(OWNERS):
            v = full[half_id, o]
            squares = squares + v * v
    squares = squares[0] + squares[1] + squares[2]
    norm = jnp.sqrt(jnp.sum(jnp.sum(squares, axis=0, keepdims=True), axis=1, keepdims=True))
    factor = jnp.minimum(1.0, CEILING / (norm + 1e-06))
    for half_id in range(2):
        cols = slice(128 * half_id, 128 * half_id + 128)
        for o in range(OWNERS):
            for q in range(2):
                row = 8 * o + 4 * q
                pg_ref[row : row + 4, cols] = full[half_id, o, q] * factor
        for o in range(16):
            row = 4 * (o % 8)
            rg_ref[o // 8, row : row + 4, cols] = full[half_id, o, 2] * factor
        sg_ref[:, cols] = full[half_id, 16, 2, 0:1, :] * factor
    writes += [write(pg_ref, pg_hbm, 2), write(rg_ref, rg_hbm, 3), write(sg_ref, sg_hbm, 4)]
    for done in writes:
        done.wait()


def shards(inputs, cotangent, decay_rate, rotation, readout, skip_gain, projection):
    bf16 = jnp.bfloat16
    row, state, square = (RUN, CHANNELS), (2, STATES, CHANNELS), (CHANNELS, CHANNELS)
    pieces = (GROUP, 16, 128)
    sums = (2, OWNERS, 3, 4, 128)
    vmem = pl.BlockSpec(memory_space=pltpu.VMEM)
    hbm = pl.BlockSpec(memory_space=pltpu.HBM)
    operands = [
        pltpu.VMEM(row, bf16), pltpu.VMEM(row, bf16), pltpu.VMEM(state[1:], F32),
        pltpu.VMEM(state[1:], F32), pltpu.VMEM(state, F32), pltpu.VMEM((1, CHANNELS), F32),
        pltpu.VMEM(square, bf16),
    ]
    shapes = [row] * 5 + [(16,) + state, state, state, pieces, pieces]
    shapes += [(2 * GROUP, 16, 128), (2,) + pieces, (2, 16, 128)] + [pieces] * 6
    shapes += [(2, OWNERS, 2, 4, 128), (2, 17, 4, 128), (OWNERS, 2, 4, 128), (17, 4, 128)]
    shapes += [sums[1:], sums[1:], (1, 3, 4, 128), (BLOCKS, 3, 4, 128)]
    out, in_grad, total = pl.pallas_call(
        kernel,
        out_shape=(
            jax.ShapeDtypeStruct(row, bf16),
            jax.ShapeDtypeStruct(row, bf16),
            jax.ShapeDtypeStruct(sums, F32),
        ),
        in_specs=[hbm] * 7,
        out_specs=[vmem] * 3,
        scratch_shapes=operands
        + [pltpu.VMEM(shape, F32) for shape in shapes]
        + [pltpu.SemaphoreType.DMA((7,)), pltpu.SemaphoreType.DMA((12,)), pltpu.SemaphoreType.DMA((12,)), pltpu.SemaphoreType.REGULAR],
        compiler_params=pltpu.CompilerParams(
            collective_id=0, has_side_effects=True, vmem_limit_bytes=32 << 20
        ),
        name="layer",
    )(
        *(
            pltpu.with_memory_space_constraint(v, pltpu.HBM)
            for v in (
                inputs[0], cotangent[0], decay_rate, rotation, readout,
                skip_gain.reshape(1, CHANNELS), projection,
            )
        )
    )
    outs = pl.pallas_call(
        finish,
        out_shape=(
            jax.ShapeDtypeStruct(row, bf16),
            jax.ShapeDtypeStruct(row, bf16),
            jax.ShapeDtypeStruct(square, F32),
            jax.ShapeDtypeStruct(state, F32),
            jax.ShapeDtypeStruct((1, CHANNELS), F32),
        ),
        in_specs=[vmem] * 3,
        out_specs=[hbm] * 5,
        scratch_shapes=[
            pltpu.VMEM(square, F32), pltpu.VMEM(state, F32), pltpu.VMEM((1, CHANNELS), F32),
            pltpu.SemaphoreType.DMA((5,)),
        ],
        compiler_params=pltpu.CompilerParams(vmem_limit_bytes=4 << 20),
        name="finish",
    )(out, in_grad, total)
    return outs[0][None], outs[1][None], outs[2], outs[3], outs[4].reshape(CHANNELS)


def solution(mesh):
    split = P("batch", "seq", None)
    return jax.shard_map(
        shards,
        mesh=mesh,
        in_specs=(split, split, P(), P(), P(), P(), P()),
        out_specs=(split, split, P(), P(), P()),
        check_vma=False,
    )
```

```python
import math

import jax
import jax.numpy as jnp
import numpy as np
from jax import lax
from jax.experimental import pallas as pl
from jax.experimental.pallas import tpu as pltpu
from jax.sharding import PartitionSpec as P

MESH = pl.DeviceIdType.MESH
F32 = jnp.float32
STATES, CHANNELS, RUN = 32, 256, 128
GROUP = 8
BLOCKS = 8
OWNERS = 32

TURN_HI = 6.28125
TURN_MID = round((2 * math.pi - TURN_HI) * 2**20) / 2**20
TURN_LO = 2 * math.pi - TURN_HI - TURN_MID
GELU_SCALE = math.sqrt(2 / math.pi)
GELU_CUBE = 0.044715
CEILING = math.sqrt(CHANNELS * CHANNELS + 2 * STATES * CHANNELS + CHANNELS)


def hops(k):
    return k // 16 + min(k // 4 % 4, 4 - k // 4 % 4) + min(k % 4, 4 - k % 4)


FAR_FIRST = sorted(range(1, OWNERS), key=lambda k: (-hops(k), k))


def cmul(a, b):
    return a[0] * b[0] - a[1] * b[1], a[0] * b[1] + a[1] * b[0]


def decay_power(decay, rotation, times):
    angle = rotation * float(times)
    if times > 1:
        turns = jnp.floor(angle * (0.5 / math.pi) + 0.5)
        angle = ((angle - turns * TURN_HI) - turns * TURN_MID) - turns * TURN_LO
    size = jnp.exp(decay * -float(times))
    return size * jnp.cos(angle), size * jnp.sin(angle)


def entry_gain(decay):
    y = 2.0 * decay
    series = 1.0 - y * (1.0 / 8)
    for k in (7, 6, 5, 4, 3, 2):
        series = 1.0 - y * (1.0 / k) * series
    return jnp.sqrt(jnp.where(y < 0.25, y * series, 1.0 - jnp.exp(-y)))


def put_pieces(ref, value):
    re, im = value
    for p in range(GROUP):
        rows, cols = slice(8 * (p // 2), 8 * (p // 2) + 8), slice(128 * (p % 2), 128 * (p % 2) + 128)
        ref[p, 0:8, :] = re[rows, cols]
        ref[p, 8:16, :] = im[rows, cols]


def get_pieces(ref):
    def part(lo):
        return jnp.concatenate(
            [
                jnp.concatenate([ref[2 * n, lo : lo + 8, :], ref[2 * n + 1, lo : lo + 8, :]], axis=1)
                for n in range(4)
            ],
            axis=0,
        )

    return part(0), part(8)


def load(ref, i):
    return ref[i, 0:8, :], ref[i, 8:16, :]


def store(ref, i, value):
    ref[i, 0:8, :] = value[0]
    ref[i, 8:16, :] = value[1]


def kernel(
    x_hbm, cot_hbm, decay_hbm, rot_hbm, read_hbm, skip_hbm, proj_hbm,
    out_ref, ig_ref, full,
    x_ref, cot_ref, decay_ref, rot_ref, read_ref, skip_ref, proj_ref,
    xf, gf, mix, hb, il,
    tab, lam_s, cof_s, l128, l1024,
    e_buf, o_buf, t_buf, r1f, r2f, hin, r1b, r2b, lin,
    pb, gb, ra1p, ra1g, a2s, ra2, pc, ra3,
    isem, ssem, rsem, far_sem,
):
    s, b = lax.axis_index("seq"), lax.axis_index("batch")
    g, blk = lax.rem(s, GROUP), lax.div(s, GROUP)
    y, c = lax.div(b, 2), lax.rem(b, 2)
    me = lax.div(g, 4) * 16 + lax.rem(g, 4) * 4 + y

    base = blk * GROUP
    zs = [lax.rem(lax.div(g, 4) + k, 2) for k in range(2)]
    xs = [lax.rem(lax.rem(g, 4) + k, 4) for k in range(4)]
    ys = [lax.rem(y + k, 4) for k in range(4)]
    seqs = [[base + z * 4 + x for x in xs] for z in zs]
    batches = [v * 2 + c for v in ys]
    in_block = [
        (zs[k // 4] * 4 + xs[k % 4], {"seq": seqs[k // 4][k % 4], "batch": b})
        for k in (6, 5, 7, 2, 4, 1, 3)
    ]
    across = [{"seq": lax.rem(blk + k, BLOCKS) * GROUP + g, "batch": b} for k in range(BLOCKS)]
    owners = [
        (
            zs[k // 16] * 16 + xs[k // 4 % 4] * 4 + ys[k % 4],
            {"seq": seqs[k // 16][k // 4 % 4], "batch": batches[k % 4]},
        )
        for k in FAR_FIRST
    ]
    other = {"seq": s, "batch": y * 2 + (1 - c)}

    fetches = [
        pltpu.make_async_copy(src, dst, isem.at[i])
        for i, (src, dst) in enumerate(
            [(decay_hbm, decay_ref), (rot_hbm, rot_ref), (read_hbm, read_ref), (x_hbm, x_ref),
             (skip_hbm, skip_ref), (cot_hbm, cot_ref), (proj_hbm, proj_ref)]
        )
    ]
    barrier = pltpu.get_barrier_semaphore()
    partners = [across[k] for k in (2, 6, 1, 7)] + [device for _, device in in_block]
    partners += [{"seq": s, "batch": batch} for batch in batches[1:]] + [other]

    def greet(sem, devices):
        for device in devices:
            pl.semaphore_signal(sem, inc=1, device_id=device, device_id_type=MESH)

    greet(barrier, partners)
    for fetch in fetches:
        fetch.start()

    def copy(src, dst, n, device):
        return pltpu.make_async_remote_copy(
            src_ref=src, dst_ref=dst, send_sem=ssem.at[n], recv_sem=rsem.at[n],
            device_id=device, device_id_type=MESH,
        )

    for fetch in fetches:
        fetch.wait()

    decay, rot = decay_ref[...], rot_ref[...]
    gain = entry_gain(decay)
    lam = decay_power(decay, rot, 1)
    lam_s[0], lam_s[1] = lam
    cof_s[0] = gain * read_ref[0]
    cof_s[1] = gain * read_ref[1]
    xf[...] = x_ref[...].astype(F32)
    row_id = lax.broadcasted_iota(jnp.int32, (8, CHANNELS), 0)
    zero = jnp.zeros((STATES, CHANNELS), F32)

    def sweep(carry, body, backward=False, lo=0, hi=RUN // 8):
        def step(i, carry):
            first = RUN - 8 - 8 * i if backward else 8 * i
            return body(pl.multiple_of(first, 8), carry)

        return lax.fori_loop(lo, hi, step, carry)

    order = tuple(range(8))

    def fwd_state(first, carry):
        lam_re, lam_im = lam_s[0], lam_s[1]
        rows = xf[pl.ds(first, 8), :]
        re, im = carry
        for j in order:
            re, im = lam_re * re - lam_im * im + rows[j : j + 1, :], lam_re * im + lam_im * re
        return re, im

    def fwd_local(first, carry):
        lam_re, lam_im = lam_s[0], lam_s[1]
        cof_re, cof_im = cof_s[0], cof_s[1]
        rows = xf[pl.ds(first, 8), :]
        re, im = carry
        acc = jnp.zeros((8, CHANNELS), F32)
        for j in order:
            re, im = lam_re * re - lam_im * im + rows[j : j + 1, :], lam_re * im + lam_im * re
            total = jnp.sum(cof_re * re - cof_im * im, axis=0, keepdims=True)
            acc = jnp.where(row_id == j, total, acc)
        mix[pl.ds(first, 8), :] = acc + rows * skip_ref[...]
        return re, im

    re, im = sweep((zero, zero), fwd_state)
    put_pieces(e_buf, (gain * re, gain * im))
    pl.semaphore_wait(barrier, len(partners))

    sends = []

    def scatter(buf, dst, n):
        dst[g] = buf[g]
        for p, device in in_block:
            copy(buf.at[p], dst.at[g], n, device).start()
        sends.append((buf.at[pl.ds(0, GROUP - 1)], n))

    def spread(src, dst, n):
        dst[blk] = src[...]
        for k in (4, 5, 3, 6, 2, 7, 1):
            copy(src, dst.at[blk], n, across[k]).start()
        sends.append((dst.at[pl.ds(0, BLOCKS - 1)], n))

    def arrive(ref, n):
        copy(ref, ref, n, other).wait_recv()

    def block_total(r1, turn):
        step = load(l128, g)
        total = load(r1, turn[0])
        for i in turn[1:]:
            moved = cmul(step, total)
            nxt = load(r1, i)
            total = moved[0] + nxt[0], moved[1] + nxt[1]
        return total

    def entering(r1, r2, buf, turn, backward):
        step, leap = load(l128, g), load(l1024, g)
        state = (jnp.zeros((8, 128), F32), jnp.zeros((8, 128), F32))
        for i in turn:
            moved, nxt = cmul(leap, state), load(r2, i)
            use = (i > blk) if backward else (i < blk)
            state = tuple(jnp.where(use, m + v, old) for m, v, old in zip(moved, nxt, state))
        for i in turn:
            store(buf, i, state)
            moved, nxt = cmul(step, state), load(r1, i)
            state = moved[0] + nxt[0], moved[1] + nxt[1]

    up, down = tuple(range(8)), tuple(range(7, -1, -1))
    seven = pl.ds(0, 7)

    greet(far_sem, (across[2], across[6]))
    scatter(e_buf, r1f, 0)
    put_pieces(l128, decay_power(decay, rot, RUN))
    put_pieces(l1024, decay_power(decay, rot, RUN * GROUP))
    sweep((zero, zero), fwd_local)
    hb[...] = lax.dot_general(
        cot_ref[...], proj_ref[...], (((1,), (1,)), ((), ())), preferred_element_type=F32
    )
    pl.semaphore_wait(far_sem, 2)
    arrive(r1f.at[seven], 0)
    t = block_total(r1f, up)
    t_buf[0, 0:8, :], t_buf[0, 8:16, :] = t
    spread(t_buf.at[0], r2f, 1)

    def fill_table(j, power):
        tab[j, 0], tab[j, 1] = power
        return cmul((lam_s[0], lam_s[1]), power)

    lax.fori_loop(0, 16, fill_table, (lam_s[0], lam_s[1]))
    gb[...] = jnp.zeros_like(gb)
    a2s[...] = jnp.zeros_like(a2s)
    arrive(r2f.at[seven], 1)
    entering(r1f, r2f, o_buf.at[0], up, False)
    scatter(o_buf.at[0], hin, 2)
    arrive(hin.at[seven], 2)

    enter = get_pieces(hin)
    carried = cmul((read_ref[0], read_ref[1]), enter)

    def inject(carried, ref, backward):
        def step(i, carry):
            re, im = carry
            for part in range(2):
                first = 16 * i + 8 * part
                acc = jnp.zeros((8, CHANNELS), F32)
                for j in order:
                    n = 8 * part + j
                    total = jnp.sum(tab[n, 0] * re - tab[n, 1] * im, axis=0, keepdims=True)
                    acc = jnp.where(row_id == (7 - j if backward else j), total, acc)
                first = pl.multiple_of(RUN - 8 - first if backward else first, 8)
                ref[pl.ds(first, 8), :] = ref[pl.ds(first, 8), :] + acc
            return cmul((tab[15, 0], tab[15, 1]), carry)

        lax.fori_loop(0, RUN // 16, step, carried)

    inject(carried, mix, False)

    mixed = mix[...]
    square = mixed * mixed
    tanh = jnp.tanh(GELU_SCALE * (mixed + GELU_CUBE * (mixed * square)))
    half = 0.5 * (1.0 + tanh)
    hidden = (mixed * half).astype(jnp.bfloat16)
    slope = half + (0.5 * mixed) * (1.0 - tanh * tanh) * (
        GELU_SCALE * (1.0 + (3.0 * GELU_CUBE) * square)
    )
    grad = hb[...] * slope
    gf[...] = grad
    part = lax.dot_general(
        hidden, cot_ref[...], (((0,), (0,)), ((), ())), preferred_element_type=F32
    )
    for half_id in range(2):
        for o in range(OWNERS):
            for q in range(2):
                row = 8 * o + 4 * q
                pb[half_id, o, q] = part[row : row + 4, 128 * half_id : 128 * half_id + 128]
    copy(pb.at[1 - c], ra1p, 3, other).start()
    sends.append((pb.at[0], 3))

    def bwd_local(first, carry):
        lam_re, lam_im = lam_s[0], lam_s[1]
        rows, xs = gf[pl.ds(first, 8), :], xf[pl.ds(first, 8), :]
        re, im, sum_re, sum_im = carry
        for j in reversed(order):
            re, im = lam_re * re - lam_im * im + rows[j : j + 1, :], lam_re * im + lam_im * re
            sum_re = sum_re + xs[j : j + 1, :] * re
            sum_im = sum_im + xs[j : j + 1, :] * im
        return re, im, sum_re, sum_im

    re, im, sum_re, sum_im = sweep((zero, zero, zero, zero), bwd_local, True)
    lam = lam_s[0], lam_s[1]
    extra = cmul(cmul(lam, (re, im)), get_pieces(hin))
    read_re = gain * sum_re + extra[0]
    read_im = -(gain * sum_im + extra[1])
    skip_part = jnp.sum(gf[...] * xf[...], axis=0, keepdims=True)
    for half_id in range(2):
        cols = slice(128 * half_id, 128 * half_id + 128)
        for o in range(16):
            gb[half_id, o] = (read_re if o < 8 else read_im)[4 * (o % 8) : 4 * (o % 8) + 4, cols]
        gb[half_id, 16, 0:1, :] = skip_part[:, cols]
    copy(gb.at[1 - c], ra1g, 5, other).start()
    sends.append((gb.at[0], 5))
    put_pieces(e_buf.at[pl.ds(GROUP, GROUP)], (re, im))
    scatter(e_buf.at[pl.ds(GROUP, GROUP)], r1b, 4)
    arrive(ra1p, 3)
    for o in range(OWNERS):
        a2s[o, 0:2] = pb[c, o] + ra1p[o]
    arrive(ra1g, 5)
    for o in range(17):
        a2s[o, 2] = gb[c, o] + ra1g[o]
    ra2[me] = a2s[me]
    for o, device in owners:
        copy(a2s.at[o], ra2.at[me], 6, device).start()
    sends.append((ra2.at[pl.ds(0, OWNERS - 1)], 6))

    arrive(r1b.at[seven], 4)
    t = block_total(r1b, down)
    t_buf[1, 0:8, :], t_buf[1, 8:16, :] = t
    spread(t_buf.at[1], r2b, 7)


    arrive(ra2.at[pl.ds(0, OWNERS - 1)], 6)
    terms = [ra2[o] for o in range(OWNERS)]
    while len(terms) > 1:
        terms = [a + b for a, b in zip(terms[::2], terms[1::2])]
    pc[0] = terms[0]
    spread(pc.at[0], ra3, 8)

    out_ref[...] = (
        xf[...] + jnp.dot(hidden, proj_ref[...], preferred_element_type=F32)
    ).astype(jnp.bfloat16)

    def bwd_read(first, carry):
        lam_re, lam_im = lam_s[0], lam_s[1]
        cof_re, cof_im = cof_s[0], cof_s[1]
        rows = gf[pl.ds(first, 8), :]
        re, im = carry
        acc = jnp.zeros((8, CHANNELS), F32)
        for j in reversed(order):
            re, im = lam_re * re - lam_im * im + rows[j : j + 1, :], lam_re * im + lam_im * re
            total = jnp.sum(cof_re * re - cof_im * im, axis=0, keepdims=True)
            acc = jnp.where(row_id == j, total, acc)
        il[pl.ds(first, 8), :] = acc + rows * skip_ref[...]
        return re, im

    sweep((zero, zero), bwd_read, True)
    il[...] = il[...] + cot_ref[...].astype(F32)

    arrive(r2b.at[seven], 7)
    entering(r1b, r2b, o_buf.at[1], down, True)
    scatter(o_buf.at[1], lin, 9)

    arrive(ra3.at[seven], 8)
    total = ra3[0]
    for o in range(1, BLOCKS):
        total = total + ra3[o]
    full[c, me] = total
    for _, device in owners:
        far = {"seq": device["seq"], "batch": device["batch"] + (1 - 2 * c)}
        copy(full.at[c, me], full.at[c, me], 11, far).start()
        copy(full.at[c, me], full.at[c, me], 10, device).start()
    copy(full.at[c, me], full.at[c, me], 11, other).start()
    sends.append((ra2.at[pl.ds(0, OWNERS - 1)], 10))

    arrive(lin.at[seven], 9)
    carried = cmul((cof_s[0], cof_s[1]), get_pieces(lin))

    inject(carried, il, True)
    ig_ref[...] = il[...].astype(jnp.bfloat16)

    arrive(full.at[c, pl.ds(0, OWNERS - 1)], 10)
    sends.append((full.at[0], 11))
    arrive(full.at[1 - c], 11)
    for ref, n in sends:
        copy(ref, ref, n, other).wait_send()


def finish(
    out_ref, ig_ref, full,
    out_hbm, ig_hbm, pg_hbm, rg_hbm, sg_hbm,
    pg_ref, rg_ref, sg_ref, sem,
):
    def write(src, dst, i):
        done = pltpu.make_async_copy(src, dst, sem.at[i])
        done.start()
        return done

    writes = [write(out_ref, out_hbm, 0), write(ig_ref, ig_hbm, 1)]
    squares = jnp.zeros((3, 4, 128), F32)
    for half_id in range(2):
        for o in range(OWNERS):
            v = full[half_id, o]
            squares = squares + v * v
    squares = squares[0] + squares[1] + squares[2]
    norm = jnp.sqrt(jnp.sum(jnp.sum(squares, axis=0, keepdims=True), axis=1, keepdims=True))
    factor = jnp.minimum(1.0, CEILING / (norm + 1e-06))
    for half_id in range(2):
        cols = slice(128 * half_id, 128 * half_id + 128)
        for o in range(OWNERS):
            for q in range(2):
                row = 8 * o + 4 * q
                pg_ref[row : row + 4, cols] = full[half_id, o, q] * factor
        for o in range(16):
            row = 4 * (o % 8)
            rg_ref[o // 8, row : row + 4, cols] = full[half_id, o, 2] * factor
        sg_ref[:, cols] = full[half_id, 16, 2, 0:1, :] * factor
    writes += [write(pg_ref, pg_hbm, 2), write(rg_ref, rg_hbm, 3), write(sg_ref, sg_hbm, 4)]
    for done in writes:
        done.wait()


def shards(inputs, cotangent, decay_rate, rotation, readout, skip_gain, projection):
    bf16 = jnp.bfloat16
    row, state, square = (RUN, CHANNELS), (2, STATES, CHANNELS), (CHANNELS, CHANNELS)
    pieces = (GROUP, 16, 128)
    sums = (2, OWNERS, 3, 4, 128)
    vmem = pl.BlockSpec(memory_space=pltpu.VMEM)
    hbm = pl.BlockSpec(memory_space=pltpu.HBM)
    operands = [
        pltpu.VMEM(row, bf16), pltpu.VMEM(row, bf16), pltpu.VMEM(state[1:], F32),
        pltpu.VMEM(state[1:], F32), pltpu.VMEM(state, F32), pltpu.VMEM((1, CHANNELS), F32),
        pltpu.VMEM(square, bf16),
    ]
    shapes = [row] * 5 + [(16,) + state, state, state, pieces, pieces]
    shapes += [(2 * GROUP, 16, 128), (2,) + pieces, (2, 16, 128)] + [pieces] * 6
    shapes += [(2, OWNERS, 2, 4, 128), (2, 17, 4, 128), (OWNERS, 2, 4, 128), (17, 4, 128)]
    shapes += [sums[1:], sums[1:], (1, 3, 4, 128), (BLOCKS, 3, 4, 128)]
    out, in_grad, total = pl.pallas_call(
        kernel,
        out_shape=(
            jax.ShapeDtypeStruct(row, bf16),
            jax.ShapeDtypeStruct(row, bf16),
            jax.ShapeDtypeStruct(sums, F32),
        ),
        in_specs=[hbm] * 7,
        out_specs=[vmem] * 3,
        scratch_shapes=operands
        + [pltpu.VMEM(shape, F32) for shape in shapes]
        + [pltpu.SemaphoreType.DMA((7,)), pltpu.SemaphoreType.DMA((12,)), pltpu.SemaphoreType.DMA((12,)), pltpu.SemaphoreType.REGULAR],
        compiler_params=pltpu.CompilerParams(
            collective_id=0, has_side_effects=True, vmem_limit_bytes=32 << 20
        ),
        name="layer",
    )(
        *(
            pltpu.with_memory_space_constraint(v, pltpu.HBM)
            for v in (
                inputs[0], cotangent[0], decay_rate, rotation, readout,
                skip_gain.reshape(1, CHANNELS), projection,
            )
        )
    )
    outs = pl.pallas_call(
        finish,
        out_shape=(
            jax.ShapeDtypeStruct(row, bf16),
            jax.ShapeDtypeStruct(row, bf16),
            jax.ShapeDtypeStruct(square, F32),
            jax.ShapeDtypeStruct(state, F32),
            jax.ShapeDtypeStruct((1, CHANNELS), F32),
        ),
        in_specs=[vmem] * 3,
        out_specs=[hbm] * 5,
        scratch_shapes=[
            pltpu.VMEM(square, F32), pltpu.VMEM(state, F32), pltpu.VMEM((1, CHANNELS), F32),
            pltpu.SemaphoreType.DMA((5,)),
        ],
        compiler_params=pltpu.CompilerParams(vmem_limit_bytes=4 << 20),
        name="finish",
    )(out, in_grad, total)
    return outs[0][None], outs[1][None], outs[2], outs[3], outs[4].reshape(CHANNELS)


def solution(mesh):
    split = P("batch", "seq", None)
    return jax.shard_map(
        shards,
        mesh=mesh,
        in_specs=(split, split, P(), P(), P(), P(), P()),
        out_specs=(split, split, P(), P(), P()),
        check_vma=False,
    )
```
